512 devices in a mesh: dp: 32 (over x, z), var: 16 (over y, core).
Axes of the slice: x: 4, y: 8, z: 8, core: 2. Of those that a mesh axis runs over, the one named last changes fastest.
Arguments:
- pixels: bfloat16 [32, 96, 4, 256], P('dp', 'var'), may hold values from -6 to 6
- var_ids: int32 [32, 96], P('dp', 'var'), may hold values from 0 to 90, as said below
- counts: int32 [32], P('dp'), may hold values from 3 to 91, as said below
- patch_weight: bfloat16 [91, 4, 1024], replicated, may hold values from -3 to 3
- var_embed: bfloat16 [91, 1024], replicated, may hold values from -5 to 5
- norm_gain: float32 [1024], replicated, may hold values from 0.1 to 1.9
- norm_bias: float32 [1024], replicated, may hold values from -3 to 3
- key_weight: bfloat16 [1024, 1024], P('dp'), may hold values from -0.1875 to 0.1875
- value_weight: bfloat16 [1024, 1024], P('dp'), may hold values from -0.1875 to 0.1875
- query: float32 [16, 64], replicated, may hold values from -200 to 200
- out_weight: bfloat16 [1024, 1024], replicated, may hold values from -0.1875 to 0.1875
Outputs:
- aggregated: bfloat16 [32, 256, 1024], P('dp', 'var')
The draws below stay inside these ranges and needn't reach their ends.
Inputs may be any that keep to these rules, and one draw needn't show every extreme that they name: `var_ids`: in each sample the ids of slots below its count are distinct; slots at or past the count are padding with arbitrary ids. `counts`: some sample has exactly min(91, 96) live slots and some has exactly 3.
All inputs are finite; a program needn't handle non-finite values.
Results may differ from the reference program's by a relative error of at most 0.018.
Values may be sent and summed in bfloat16 or wider, within the bound.
No kernel may reach another device: no remote copies, remote signals or barrier semaphores. Data moves between devices by JAX's collectives and lax.ppermute only.
A program may use at most 64 MiB of HBM per device.

```python
import math
import jax
import jax.numpy as jnp
from jax import lax

D = 1024
HEADS = 16
HEAD = 64
PP = 4
VARS = 91
PW = 256
BATCH = 32
VSLOTS = 96


def draw_var_ids(key, part):
    sample_keys = jax.random.split(key, BATCH)

    def one(sample_key):
        order = jax.random.permutation(sample_key, VARS).astype(jnp.int32)
        filler = jax.random.randint(jax.random.fold_in(sample_key, 7), (VSLOTS,), 0, VARS).astype(jnp.int32)
        return jnp.concatenate([order, filler])[:VSLOTS]
    return jax.vmap(one)(sample_keys)


def draw_counts(key, part):
    highest = min(VARS, VSLOTS)
    base = jax.random.randint(jax.random.fold_in(key, 11), (BATCH,), 3, highest + 1).astype(jnp.int32)
    picked = jax.random.permutation(jax.random.fold_in(key, 13), BATCH)
    base = jnp.where(picked == 0, jnp.int32(highest), base)
    base = jnp.where(picked == 1, jnp.int32(3), base)
    return base.astype(jnp.int32)


def draw_query(key, part):
    first = jax.random.fold_in(key, 21)
    second = jax.random.fold_in(key, 23)
    base = jnp.clip(jax.random.normal(first, (HEADS, HEAD), jnp.float32), -5.0, 5.0)
    scales = jnp.exp(jax.random.uniform(second, (HEADS, 1), jnp.float32, math.log(0.5), math.log(4.0)))
    return (base * scales).astype(jnp.float32)


def block_levels(rng, extent, pieces, least, top_value):
    gain, own = 1.0, jax.random.fold_in(rng, 6)
    for position, blocks in pieces:
        heights = jnp.exp(jax.random.uniform(jax.random.fold_in(own, position), (blocks,), jnp.float32, least / len(pieces), top_value / len(pieces)))
        gain = gain * jnp.repeat(heights, extent[position] // blocks).reshape([-1 if axis == position else 1 for axis in range(len(extent))])
    return gain


def bell_draw(rng, dims, width, reach, cuts=(), kind=jnp.bfloat16):
    factor_of = block_levels(rng, dims, cuts, -0.22, 0.18) if cuts else 1.0
    values = jax.random.normal(rng, dims, jnp.float32) * width * factor_of
    return jnp.minimum(jnp.maximum(values, -reach), reach).astype(kind)


def setup_inputs(seed: int = 0) -> dict:
    splits = jax.random.split(jax.random.key(seed), 12)
    pixels = bell_draw(splits[0], (BATCH, VSLOTS, PP, PW), 1.0, 6.0, ((0, 32), (1, 16)))
    var_ids = draw_var_ids(jax.random.fold_in(splits[11], 71), 0)
    counts = draw_counts(jax.random.fold_in(splits[11], 71), 0)
    patch_weight = bell_draw(splits[3], (VARS, PP, D), PP ** -0.5, 3.0)
    var_embed = bell_draw(splits[4], (VARS, D), 1.0, 5.0)
    norm_gain = jnp.clip(1.0 + 0.18 * jax.random.normal(splits[5], (D,), jnp.float32), 0.1, 1.9)
    norm_bias = bell_draw(splits[6], (D,), 0.5, 3.0, (), jnp.float32)
    key_weight = bell_draw(splits[7], (D, D), D ** -0.5, 0.1875, ((0, 32),))
    value_weight = bell_draw(splits[8], (D, D), D ** -0.5, 0.1875, ((0, 32),))
    query = draw_query(jax.random.fold_in(splits[11], 71), 0)
    out_weight = bell_draw(splits[10], (D, D), D ** -0.5, 0.1875)
    return {"pixels": pixels, "var_ids": var_ids, "counts": counts, "patch_weight": patch_weight, "var_embed": var_embed, "norm_gain": norm_gain, "norm_bias": norm_bias, "key_weight": key_weight, "value_weight": value_weight, "query": query, "out_weight": out_weight}


def one_sample(pixels, ids, count, patch_weight, var_embed, norm_gain, norm_bias, key_weight, value_weight, query, out_weight):
    table = patch_weight[ids]
    embedded = jnp.einsum('skp,skd->spd', pixels.astype(jnp.float32), table.astype(jnp.float32))
    embedded = embedded + var_embed[ids].astype(jnp.float32)[:, None, :]
    center = embedded - lax.optimization_barrier(jnp.mean(embedded, axis=-1, keepdims=True))
    spread = lax.optimization_barrier(jnp.mean(center * center, axis=-1, keepdims=True))
    normed = (center * lax.rsqrt(spread + 1e-05) * norm_gain + norm_bias).astype(jnp.bfloat16)
    slots = normed.shape[0]
    patches = normed.shape[1]
    flat = normed.reshape(slots * patches, D)
    keys = jnp.dot(flat, key_weight, preferred_element_type=jnp.float32).reshape(slots * patches, HEADS, HEAD)
    scores = jnp.einsum('nhe,he->nh', keys, query, precision=lax.Precision.HIGHEST) * (1.0 / math.sqrt(HEAD))
    scores = scores.reshape(slots, patches, HEADS)
    live = (jnp.arange(slots, dtype=jnp.int32) < count)[:, None, None]
    scores = jnp.where(live, scores, jnp.float32(-1e+30))
    peak = lax.optimization_barrier(jnp.max(scores, axis=0))
    expo = jnp.exp(scores - peak)
    total = lax.optimization_barrier(jnp.sum(expo, axis=0))
    probs = expo.astype(jnp.bfloat16)
    values = jnp.dot(flat, value_weight, preferred_element_type=jnp.float32).astype(jnp.bfloat16)
    values = values.reshape(slots, patches, HEADS, HEAD)
    numer = jnp.einsum('sph,sphe->phe', probs.astype(jnp.float32), values.astype(jnp.float32))
    mixed = (numer / total[:, :, None]).reshape(patches, D).astype(jnp.bfloat16)
    return jnp.dot(mixed, out_weight, preferred_element_type=jnp.float32).astype(jnp.bfloat16)

def reference(pixels, var_ids, counts, patch_weight, var_embed, norm_gain, norm_bias, key_weight, value_weight, query, out_weight):

    def apply(item):
        return one_sample(item[0], item[1], item[2], patch_weight, var_embed, norm_gain, norm_bias, key_weight, value_weight, query, out_weight)
    return lax.map(apply, (pixels, var_ids, counts))
```

```python
import math

import jax
import jax.numpy as jnp
from jax import lax
from jax.experimental import pallas as pl
from jax.experimental.pallas import tpu as pltpu
from jax.sharding import Mesh
from jax.sharding import PartitionSpec as P

DP = ("dp_0", "dp_1")
F32 = jnp.float32
BF16 = jnp.bfloat16
PAIRS = [(k, l) for k in range(5) for l in range(k, 5)]


def whole(memory_space=pltpu.VMEM):
    return pl.BlockSpec(memory_space=memory_space)


def iota(shape, dim):
    return lax.broadcasted_iota(jnp.int32, shape, dim)


def head_slice_kernel(var_ref, wk_ref, wv_ref, out_ref):
    head = var_ref[0]
    at = pl.multiple_of((head // 2) * 128, 128)
    half = head % 2
    wk = wk_ref[:, pl.ds(at, 128)].astype(F32)
    wv = wv_ref[:, pl.ds(at, 128)].astype(F32)
    lane = iota(wk.shape, 1)
    both = jnp.where(lane // 64 == half, wv, pltpu.roll(wk, 64, 1)).astype(BF16)
    for d in range(out_ref.shape[0]):
        out_ref[d] = both


def table_kernel(ids_ref, pix_ref, pw_ref, ve_ref, gain_ref, bias_ref, hi_ref, lo_ref, send_ref, ac, af, rows, chunk):
    n_pw, width = pw_ref.shape
    n_ve = ve_ref.shape[0]
    total = af.shape[0]
    at = n_pw + 4
    gain = gain_ref[...]

    def centered(x):
        return x - jnp.mean(x, axis=-1, keepdims=True)

    pw = centered(pw_ref[...].astype(F32))
    ac[0:n_pw, :] = pw
    af[0:n_pw, :] = pw * gain
    af[n_pw:at, :] = jnp.zeros((at - n_pw, width), F32)
    ve = centered(ve_ref[...].astype(F32))
    ac[at : at + n_ve, :] = ve
    af[at : at + n_ve, :] = ve * gain
    af[at + n_ve : at + n_ve + 1, :] = bias_ref[...]
    af[at + n_ve + 1 : total, :] = jnp.zeros((total - at - n_ve - 1, width), F32)
    a = af[...]
    hi = a.astype(BF16)
    hi_ref[...] = hi
    lo_ref[...] = (a - hi.astype(F32)).astype(BF16)

    slots = ids_ref.shape[1]
    rows[...] = jnp.zeros(rows.shape, F32)
    sub = iota((8, 256), 0)
    lane = iota((8, 256), 1)
    meta = jnp.zeros((8, 256), F32)
    for s in range(slots):
        v = ids_ref[0, s]
        for k in range(4):
            rows[k, s : s + 1, :] = ac[pl.ds(4 * v + k, 1), :]
        rows[4, s : s + 1, :] = ac[pl.ds(at + v, 1), :]
        meta = jnp.where((sub == s) & (lane == 48), v.astype(F32), meta)
    for i, (k, l) in enumerate(PAIRS):
        g = jnp.sum(rows[k] * rows[l], axis=-1, keepdims=True) * ((1.0 if k == l else 2.0) / width)
        for part in range(3):
            top = g.astype(BF16).astype(F32)
            meta = jnp.where(lane == 16 * part + i, top, meta)
            g = g - top
    chunk[0 : 4 * slots, :] = pix_ref[...].astype(F32)
    chunk[4 * slots :, :] = meta
    packed = chunk[...].astype(BF16)
    for j in range(send_ref.shape[0]):
        send_ref[j] = packed


def project_kernel(hi_ref, lo_ref, w_ref, thi_ref, tlo_ref):
    w = w_ref[...]
    t = jnp.dot(hi_ref[...], w, preferred_element_type=F32)
    t = t + jnp.dot(lo_ref[...], w, preferred_element_type=F32)
    hi = t.astype(BF16)
    thi_ref[...] = hi
    tlo_ref[...] = (t - hi.astype(F32)).astype(BF16)


def attend_kernel(var_ref, count_ref, x_ref, thi_ref, tlo_ref, query_ref, out_ref, w_scr, v_scr):
    head = var_ref[0]
    count = count_ref[0]
    half = head % 2
    slots = w_scr.shape[0] // 5
    entries = thi_ref.shape[0]
    n_pw = 364
    at = n_pw + 4
    x = x_ref[...]
    n_rows = x.shape[0]

    n = iota((slots, n_rows), 0)
    group = (n * 43) >> 8
    base = group * 32
    within = n - group * 6
    col = iota((slots, n_rows), 1)

    def picked(target):
        p = jnp.where(col == target, 1.0, 0.0).astype(BF16)
        return p

    meta = jnp.dot(picked(base + 24 + within), x[:, :128], preferred_element_type=F32)
    c = [jnp.dot(picked(base + within * 4 + k), x, preferred_element_type=F32) for k in range(4)]
    gram = meta + pltpu.roll(meta, 112, 1) + pltpu.roll(meta, 96, 1)
    ids = meta[:, 48:49].astype(jnp.int32)

    col = iota((slots, entries), 1)
    lane = iota((slots, 128), 1)
    is_value = lane // 64 == half
    q = query_ref[pl.ds(head, 1), :] * (1.0 / math.sqrt(query_ref.shape[1]))
    q2 = jnp.concatenate([q, q], axis=1)
    thi, tlo = thi_ref[...], tlo_ref[...]
    keyed = []
    for k in range(5):
        target = 4 * ids + k if k < 4 else at + ids
        pick = jnp.where(col == target, 1.0, 0.0).astype(BF16)
        thi_k = jnp.dot(pick, thi, preferred_element_type=F32)
        t_k = thi_k + jnp.dot(pick, tlo, preferred_element_type=F32)
        keyed.append(jnp.sum(jnp.where(is_value, 0.0, t_k * q2), axis=1, keepdims=True))
        v_scr[k * slots : (k + 1) * slots, :] = jnp.where(is_value, t_k, 0.0).astype(BF16)
    last = entries - 16
    tail = thi[last:, :].astype(F32) + tlo[last:, :].astype(F32)
    bias_row = tail[at + 91 - last : at + 92 - last, :]
    is_value_row = is_value[0:1, :]
    key_bias = jnp.sum(jnp.where(is_value_row, 0.0, bias_row * q2), axis=1, keepdims=True)
    value_bias = jnp.where(is_value_row, bias_row, 0.0)

    def g(k, l):
        i = PAIRS.index((k, l))
        return gram[:, i : i + 1]

    spread = g(4, 4)
    for k in range(4):
        inner = g(k, 4)
        for l in range(k, 4):
            inner = inner + g(k, l) * c[l]
        spread = spread + c[k] * inner
    r = lax.rsqrt(jnp.maximum(spread, 0.0) + 1e-05)
    dots = keyed[4]
    for k in range(4):
        dots = dots + c[k] * keyed[k]
    scores = r * dots + key_bias
    scores = jnp.where(iota(scores.shape, 0) < count, scores, -1e30)
    peak = jnp.max(scores, axis=0, keepdims=True)
    expo = jnp.exp(scores - peak)
    share = expo * (1.0 / jnp.sum(expo, axis=0, keepdims=True)) * r
    for k in range(4):
        w_scr[k * slots : (k + 1) * slots, :] = (share * c[k]).astype(BF16)
    w_scr[4 * slots :, :] = share.astype(BF16)
    mixed = lax.dot_general(
        w_scr[...], v_scr[...], (((0,), (0,)), ((), ())), preferred_element_type=F32
    )
    out_ref[...] = (mixed + value_bias).astype(BF16)


def project_out_kernel(m_ref, wo_ref, out_ref):
    parts = [m_ref[2 * i].astype(F32) + m_ref[2 * i + 1].astype(F32) for i in range(m_ref.shape[0] // 2)]
    mixed = jnp.concatenate(parts, axis=1).astype(BF16)
    out_ref[...] = jnp.dot(mixed, wo_ref[...], preferred_element_type=F32).astype(BF16)


def cost(flops, moved):
    return pl.CostEstimate(flops=flops, transcendentals=0, bytes_accessed=moved)


def on_device(
    pixels,
    var_ids,
    counts,
    patch_weight,
    var_embed,
    norm_gain,
    norm_bias,
    key_weight,
    value_weight,
    query,
    out_weight,
):
    slots, pp, patches = pixels.shape[1:]
    n_var, width = var_embed.shape
    n_dp = lax.axis_size(DP)
    n_sv = lax.axis_size("var")
    all_slots = slots * n_sv
    entries = 464
    smem, vmem = whole(pltpu.SMEM), whole()
    var = lax.axis_index("var").astype(jnp.int32).reshape(1)

    slices = pl.pallas_call(
        head_slice_kernel,
        out_shape=jax.ShapeDtypeStruct((n_dp, key_weight.shape[0], 128), BF16),
        in_specs=[smem, vmem, vmem],
        out_specs=vmem,
        name="head_slice",
    )(var, key_weight, value_weight)
    weights = lax.all_to_all(slices, DP, 0, 0, tiled=True)

    hi, lo, send = pl.pallas_call(
        table_kernel,
        out_shape=(
            jax.ShapeDtypeStruct((entries, width), BF16),
            jax.ShapeDtypeStruct((entries, width), BF16),
            jax.ShapeDtypeStruct((n_sv, 32, patches), BF16),
        ),
        in_specs=[smem] + [vmem] * 5,
        out_specs=(vmem, vmem, vmem),
        scratch_shapes=[
            pltpu.VMEM((entries, width), F32),
            pltpu.VMEM((entries, width), F32),
            pltpu.VMEM((5, 8, width), F32),
            pltpu.VMEM((32, patches), F32),
        ],
        cost_estimate=cost(20 * entries * width, 8 * entries * width),
        compiler_params=pltpu.CompilerParams(vmem_limit_bytes=24 << 20),
        name="tables",
    )(
        var_ids,
        pixels.reshape(slots * pp, patches),
        patch_weight.reshape(n_var * pp, width),
        var_embed,
        norm_gain.reshape(1, width),
        norm_bias.reshape(1, width),
    )
    weights, send = lax.optimization_barrier((weights, send))
    gathered = lax.all_to_all(send, "var", 0, 0, tiled=True)

    thi, tlo = pl.pallas_call(
        project_kernel,
        out_shape=(jax.ShapeDtypeStruct((entries, 128), BF16),) * 2,
        in_specs=[vmem] * 3,
        out_specs=(vmem, vmem),
        cost_estimate=cost(4 * entries * width * 128, 5 * entries * width),
        compiler_params=pltpu.CompilerParams(vmem_limit_bytes=16 << 20),
        name="project",
    )(hi, lo, weights.reshape(width, 128))

    mixed = pl.pallas_call(
        attend_kernel,
        out_shape=jax.ShapeDtypeStruct((patches, 128), BF16),
        in_specs=[smem, smem, vmem, vmem, vmem, vmem],
        out_specs=vmem,
        scratch_shapes=[
            pltpu.VMEM((5 * all_slots, patches), BF16),
            pltpu.VMEM((5 * all_slots, 128), BF16),
        ],
        compiler_params=pltpu.CompilerParams(vmem_limit_bytes=24 << 20),
        name="attend",
    )(var, counts, gathered.reshape(n_sv * 32, patches), thi, tlo, query)
    owned = lax.all_to_all(mixed.reshape(n_sv, patches // n_sv, 128), "var", 0, 0, tiled=True)

    out = pl.pallas_call(
        project_out_kernel,
        out_shape=jax.ShapeDtypeStruct((patches // n_sv, width), BF16),
        in_specs=[vmem, vmem],
        out_specs=vmem,
        compiler_params=pltpu.CompilerParams(vmem_limit_bytes=16 << 20),
        name="project_out",
    )(owned, out_weight)
    return out[None]


def solution(mesh):
    torus = Mesh(mesh.devices.reshape(4, 8, mesh.shape["var"]), ("dp_0", "dp_1", "var"))
    return jax.shard_map(
        on_device,
        mesh=torus,
        in_specs=(
            P(DP, "var", None, None),
            P(DP, "var"),
            P(DP),
            P(),
            P(),
            P(),
            P(),
            P(DP, None),
            P(DP, None),
            P(),
            P(),
        ),
        out_specs=P(DP, "var", None),
        check_vma=False,
    )
```

```python
import jax
import jax.numpy as jnp
from jax import lax
from jax.experimental import pallas as pl
from jax.experimental.pallas import tpu as pltpu
from jax.sharding import Mesh
from jax.sharding import PartitionSpec as P

DP = ("dp_0", "dp_1")
VAR = ("y", "core")
F32 = jnp.float32
BF16 = jnp.bfloat16
PAIRS = [(k, l) for k in range(5) for l in range(k, 5)]


def whole(memory_space=pltpu.VMEM):
    return pl.BlockSpec(memory_space=memory_space)


def iota(shape, dim):
    return lax.broadcasted_iota(jnp.int32, shape, dim)


def split3(x):
    top = x.astype(BF16).astype(F32)
    mid = (x - top).astype(BF16).astype(F32)
    return top, mid, (x - top - mid).astype(BF16).astype(F32)


def head_slice_kernel(chip_ref, wk_ref, wv_ref, query_ref, out_ref, prod):
    chip = chip_ref[0]
    at = pl.multiple_of(chip * 128, 128)
    rows = wk_ref.shape[0]
    q = query_ref[pl.ds(2 * chip, 2), :]
    q2 = jnp.concatenate([q[0:1], q[1:2]], axis=1)
    prod[...] = jnp.zeros(prod.shape, F32)
    prod[0:rows, :] = wk_ref[:, pl.ds(at, 128)].astype(F32) * q2
    sub, lane = iota((8, 128), 0), iota((8, 128), 1)
    mine = jnp.where(lane // 64 == sub % 2, 1.0, 0.0)
    fold = lax.dot_general(
        mine, prod[...], (((1,), (1,)), ((), ())), precision=lax.Precision.HIGHEST, preferred_element_type=F32
    )
    top, mid, low = split3(fold)
    part = jnp.where(sub < 2, top, jnp.where(sub < 4, mid, jnp.where(sub < 6, low, 0.0)))
    both = jnp.concatenate([wv_ref[:, pl.ds(at, 128)].astype(F32), part], axis=0).astype(BF16)
    for d in range(out_ref.shape[0]):
        out_ref[d] = both


def table_kernel(ids_ref, pix_ref, pw_ref, ve_ref, gain_ref, bias_ref, hi_ref, lo_ref, send_ref, ac, af, rows, chunk):
    n_pw, width = pw_ref.shape
    n_ve = ve_ref.shape[0]
    total = af.shape[0]
    at = n_pw + 4
    gain = gain_ref[...]

    def centered(x):
        return x - jnp.mean(x, axis=-1, keepdims=True)

    pw = centered(pw_ref[...].astype(F32))
    ac[0:n_pw, :] = pw
    af[0:n_pw, :] = pw * gain
    af[n_pw:at, :] = jnp.zeros((at - n_pw, width), F32)
    ve = centered(ve_ref[...].astype(F32))
    ac[at : at + n_ve, :] = ve
    af[at : at + n_ve, :] = ve * gain
    af[at + n_ve : at + n_ve + 1, :] = bias_ref[...]
    af[at + n_ve + 1 : total, :] = jnp.zeros((total - at - n_ve - 1, width), F32)
    a = af[...]
    hi = a.astype(BF16)
    hi_ref[...] = hi
    lo_ref[...] = (a - hi.astype(F32)).astype(BF16)

    slots = ids_ref.shape[1]
    rows[...] = jnp.zeros(rows.shape, F32)
    sub = iota((8, 128), 0)
    lane = iota((8, 128), 1)
    meta = jnp.zeros((8, 128), F32)
    for s in range(slots):
        v = ids_ref[0, s]
        for k in range(4):
            rows[k, s : s + 1, :] = ac[pl.ds(4 * v + k, 1), :]
        rows[4, s : s + 1, :] = ac[pl.ds(at + v, 1), :]
        meta = jnp.where((sub == s) & (lane == 48), v.astype(F32), meta)
    for i, (k, l) in enumerate(PAIRS):
        g = jnp.sum(rows[k] * rows[l], axis=-1, keepdims=True) * ((1.0 if k == l else 2.0) / width)
        for part, value in enumerate(split3(g)):
            meta = jnp.where(lane == 16 * part + i, value, meta)
    n = 4 * slots
    for half in range(2):
        chunk[32 * half : 32 * half + n, :] = pix_ref[:, 128 * half : 128 * half + 128].astype(F32)
        chunk[32 * half + n : 32 * half + 32, :] = meta
    send_ref[...] = chunk[...].astype(BF16)


def project_kernel(hi_ref, lo_ref, both_ref, thi_ref, tlo_ref, key_ref, w_scr, f_scr):
    n_dp = both_ref.shape[1]
    rows = both_ref.shape[2] - 8
    per = 128 // rows
    for d in range(n_dp):
        w_scr[d * rows : (d + 1) * rows, :] = both_ref[0, d, 0:rows, :]
    for i in range(n_dp // per):
        tile = jnp.zeros((8, 128), F32)
        for p in range(per):
            piece = both_ref[0, i * per + p, rows : rows + 8, :].astype(F32)
            tile = tile + (pltpu.roll(piece, rows * p, 1) if p else piece)
        f_scr[:, 128 * i : 128 * i + 128] = tile.astype(BF16)
    hi, lo = hi_ref[...], lo_ref[...]
    w, f = w_scr[...], f_scr[...]
    t = jnp.dot(hi, w, preferred_element_type=F32) + jnp.dot(lo, w, preferred_element_type=F32)
    top = t.astype(BF16)
    thi_ref[...] = top
    tlo_ref[...] = (t - top.astype(F32)).astype(BF16)
    dims = (((1,), (1,)), ((), ()))
    keys = lax.dot_general(f, hi, dims, preferred_element_type=F32)
    keys = keys + lax.dot_general(f, lo, dims, preferred_element_type=F32)
    key_ref[...] = keys + pltpu.roll(keys, 6, 0) + pltpu.roll(keys, 4, 0)


def attend_kernel(half_ref, count_ref, both_ref, thi_ref, tlo_ref, key_ref, out_ref, w_scr, v_scr):
    half = half_ref[0]
    count = count_ref[0]
    slots = w_scr.shape[0] // 5
    entries = thi_ref.shape[0]
    n_pw = 364
    at = n_pw + 4
    n_sv = slots // 6
    x = both_ref[1, 0 : 64 * n_sv, :].reshape(n_sv, 2, 32, 128)
    x = jnp.concatenate([x[:, i].reshape(32 * n_sv, 128) for i in range(2)], axis=1)
    n_rows = x.shape[0]

    n = iota((slots, n_rows), 0)
    group = (n * 43) >> 8
    base = group * 32
    within = n - group * 6
    col = iota((slots, n_rows), 1)

    def picked(target):
        p = jnp.where(col == target, 1.0, 0.0).astype(BF16)
        return p

    meta = jnp.dot(picked(base + 24 + within), x[:, :128], preferred_element_type=F32)
    c = [jnp.dot(picked(base + within * 4 + k), x, preferred_element_type=F32) for k in range(4)]
    gram = meta + pltpu.roll(meta, 112, 1) + pltpu.roll(meta, 96, 1)
    ids = meta[:, 48:49].astype(jnp.int32)

    col = iota((slots, entries), 1)
    lane = iota((slots, 128), 1)
    is_value = lane // 64 == half
    key_row = jnp.where(half == 0, key_ref[0:1, :], key_ref[1:2, :]) * 0.125
    thi, tlo = thi_ref[...], tlo_ref[...]
    keyed = []
    for k in range(5):
        target = 4 * ids + k if k < 4 else at + ids
        hit = col == target
        keyed.append(jnp.sum(jnp.where(hit, key_row, 0.0), axis=1, keepdims=True))
        pick = jnp.where(hit, 1.0, 0.0).astype(BF16)
        thi_k = jnp.dot(pick, thi, preferred_element_type=F32)
        t_k = thi_k + jnp.dot(pick, tlo, preferred_element_type=F32)
        v_scr[k * slots : (k + 1) * slots, :] = jnp.where(is_value, t_k, 0.0).astype(BF16)
    last = entries - 16
    tail = thi[last:, :].astype(F32) + tlo[last:, :].astype(F32)
    bias_row = tail[at + 91 - last : at + 92 - last, :]
    is_value_row = is_value[0:1, :]
    key_bias = key_row[:, at + 91 : at + 92]
    value_bias = jnp.where(is_value_row, bias_row, 0.0)

    def g(k, l):
        i = PAIRS.index((k, l))
        return gram[:, i : i + 1]

    spread = g(4, 4)
    for k in range(4):
        inner = g(k, 4)
        for l in range(k, 4):
            inner = inner + g(k, l) * c[l]
        spread = spread + c[k] * inner
    r = lax.rsqrt(jnp.maximum(spread, 0.0) + 1e-05)
    dots = keyed[4]
    for k in range(4):
        dots = dots + c[k] * keyed[k]
    scores = r * dots + key_bias
    scores = jnp.where(iota(scores.shape, 0) < count, scores, -1e30)
    peak = jnp.max(scores, axis=0, keepdims=True)
    expo = jnp.exp(scores - peak)
    share = expo * (1.0 / jnp.sum(expo, axis=0, keepdims=True)) * r
    for k in range(4):
        w_scr[k * slots : (k + 1) * slots, :] = (share * c[k]).astype(BF16)
    w_scr[4 * slots :, :] = share.astype(BF16)
    mixed = lax.dot_general(
        w_scr[...], v_scr[...], (((0,), (0,)), ((), ())), preferred_element_type=F32
    )
    out_ref[...] = (mixed + value_bias).astype(BF16)


def project_out_kernel(m_ref, wo_ref, out_ref):
    parts = [m_ref[2 * i].astype(F32) + m_ref[2 * i + 1].astype(F32) for i in range(m_ref.shape[0] // 2)]
    mixed = jnp.concatenate(parts, axis=1).astype(BF16)
    out_ref[...] = jnp.dot(mixed, wo_ref[...], preferred_element_type=F32).astype(BF16)


def cost(flops, moved):
    return pl.CostEstimate(flops=flops, transcendentals=0, bytes_accessed=moved)


def on_device(
    pixels,
    var_ids,
    counts,
    patch_weight,
    var_embed,
    norm_gain,
    norm_bias,
    key_weight,
    value_weight,
    query,
    out_weight,
):
    slots, pp, patches = pixels.shape[1:]
    n_var, width = var_embed.shape
    n_dp = lax.axis_size(DP)
    n_chip, n_core = lax.axis_size("y"), lax.axis_size("core")
    n_sv = n_chip * n_core
    all_slots = slots * n_sv
    entries = 464
    rows = key_weight.shape[0] + 8
    smem, vmem = whole(pltpu.SMEM), whole()
    chip = lax.axis_index("y").astype(jnp.int32).reshape(1)
    core = lax.axis_index("core").astype(jnp.int32).reshape(1)

    slices = pl.pallas_call(
        head_slice_kernel,
        out_shape=jax.ShapeDtypeStruct((n_dp, rows, 128), BF16),
        in_specs=[smem, vmem, vmem, vmem],
        out_specs=vmem,
        scratch_shapes=[pltpu.VMEM((128, 128), F32)],
        name="head_slice",
    )(chip, key_weight, value_weight, query)

    hi, lo, packed = pl.pallas_call(
        table_kernel,
        out_shape=(
            jax.ShapeDtypeStruct((entries, width), BF16),
            jax.ShapeDtypeStruct((entries, width), BF16),
            jax.ShapeDtypeStruct((64, 128), BF16),
        ),
        in_specs=[smem] + [vmem] * 5,
        out_specs=(vmem, vmem, vmem),
        scratch_shapes=[
            pltpu.VMEM((entries, width), F32),
            pltpu.VMEM((entries, width), F32),
            pltpu.VMEM((5, 8, width), F32),
            pltpu.VMEM((64, 128), F32),
        ],
        cost_estimate=cost(20 * entries * width, 8 * entries * width),
        compiler_params=pltpu.CompilerParams(vmem_limit_bytes=24 << 20),
        name="tables",
    )(
        var_ids,
        pixels.reshape(slots * pp, patches),
        patch_weight.reshape(n_var * pp, width),
        var_embed,
        norm_gain.reshape(1, width),
        norm_bias.reshape(1, width),
    )
    of_chip = lax.all_gather(packed, "core")

    def weights_of_all(slices, of_chip):
        return lax.all_to_all(slices, DP, 0, 0, tiled=True)

    def pixels_of_all(slices, of_chip):
        send = jnp.broadcast_to(of_chip, (n_chip, *of_chip.shape))
        got = lax.all_to_all(send, "y", 0, 0, tiled=True).reshape(-1, 128)
        return jnp.pad(got, ((0, n_dp * rows - got.shape[0]), (0, 0))).reshape(n_dp, rows, 128)

    mine = lax.cond(core[0] == 0, weights_of_all, pixels_of_all, slices, of_chip)
    both = lax.all_gather(mine, "core")

    thi, tlo, keys = pl.pallas_call(
        project_kernel,
        out_shape=(
            jax.ShapeDtypeStruct((entries, 128), BF16),
            jax.ShapeDtypeStruct((entries, 128), BF16),
            jax.ShapeDtypeStruct((8, entries), F32),
        ),
        in_specs=[vmem] * 3,
        out_specs=(vmem, vmem, vmem),
        scratch_shapes=[pltpu.VMEM((width, 128), BF16), pltpu.VMEM((8, width), BF16)],
        cost_estimate=cost(4 * entries * width * 128, 5 * entries * width),
        compiler_params=pltpu.CompilerParams(vmem_limit_bytes=16 << 20),
        name="project",
    )(hi, lo, both)

    mixed = pl.pallas_call(
        attend_kernel,
        out_shape=jax.ShapeDtypeStruct((patches, 128), BF16),
        in_specs=[smem, smem, vmem, vmem, vmem, vmem],
        out_specs=vmem,
        scratch_shapes=[
            pltpu.VMEM((5 * all_slots, patches), BF16),
            pltpu.VMEM((5 * all_slots, 128), BF16),
        ],
        compiler_params=pltpu.CompilerParams(vmem_limit_bytes=24 << 20),
        name="attend",
    )(core, counts, both.reshape(n_core, n_dp * rows, 128), thi, tlo, keys)
    owned = lax.all_to_all(mixed.reshape(n_sv, patches // n_sv, 128), VAR, 0, 0, tiled=True)

    out = pl.pallas_call(
        project_out_kernel,
        out_shape=jax.ShapeDtypeStruct((patches // n_sv, width), BF16),
        in_specs=[vmem, vmem],
        out_specs=vmem,
        compiler_params=pltpu.CompilerParams(vmem_limit_bytes=16 << 20),
        name="project_out",
    )(owned, out_weight)
    return out[None]


def solution(mesh):
    torus = Mesh(mesh.devices.reshape(4, 8, 8, 2), (*DP, *VAR))
    return jax.shard_map(
        on_device,
        mesh=torus,
        in_specs=(
            P(DP, VAR, None, None),
            P(DP, VAR),
            P(DP),
            P(),
            P(),
            P(),
            P(),
            P(DP, None),
            P(DP, None),
            P(),
            P(),
        ),
        out_specs=P(DP, VAR, None),
        check_vma=False,
    )
```

```python
import jax
import jax.numpy as jnp
from jax import lax
from jax.experimental import pallas as pl
from jax.experimental.pallas import tpu as pltpu
from jax.sharding import Mesh
from jax.sharding import PartitionSpec as P

DP = ("dp_0", "dp_1")
VAR = ("y", "core")
F32 = jnp.float32
BF16 = jnp.bfloat16
NT = (((1,), (1,)), ((), ()))
TN = (((0,), (0,)), ((), ()))
PAIRS = [(k, l) for k in range(5) for l in range(k, 5)]


def whole(memory_space=pltpu.VMEM):
    return pl.BlockSpec(memory_space=memory_space)


def iota(shape, dim):
    return lax.broadcasted_iota(jnp.int32, shape, dim)


def split3(x):
    top = x.astype(BF16).astype(F32)
    mid = (x - top).astype(BF16).astype(F32)
    return top, mid, (x - top - mid).astype(BF16).astype(F32)


def pack_kernel(chip_ref, ids_ref, wk_ref, wv_ref, query_ref, pix_ref, w_ref, send_ref, wk, wv, q_scr, pix, prod, chunk, sems):
    chip = chip_ref[0]
    at = pl.multiple_of(chip * 128, 128)
    copies = [
        pltpu.make_async_copy(pix_ref, pix, sems.at[0]),
        pltpu.make_async_copy(query_ref, q_scr, sems.at[1]),
        pltpu.make_async_copy(wk_ref.at[:, pl.ds(at, 128)], wk, sems.at[2]),
        pltpu.make_async_copy(wv_ref.at[:, pl.ds(at, 128)], wv, sems.at[3]),
    ]
    for copy in copies:
        copy.start()
    rows = wk.shape[0]
    slots = ids_ref.shape[1]
    prod[...] = jnp.zeros(prod.shape, F32)
    sub, lane = iota((8, 128), 0), iota((8, 128), 1)
    mine = jnp.where(lane // 64 == sub % 2, 1.0, 0.0)
    meta = jnp.zeros((8, 128), F32)
    for s in range(slots):
        meta = jnp.where(sub == s, ids_ref[0, s].astype(F32), meta)
    n = 4 * slots
    for half in range(2):
        chunk[32 * half + n : 32 * half + 32, :] = meta
    copies[0].wait()
    for s in range(slots):
        x = pix[0, s].astype(F32)
        for half in range(2):
            chunk[32 * half + 4 * s : 32 * half + 4 * s + 4, :] = x[:, 128 * half : 128 * half + 128]
    send_ref[...] = chunk[...].astype(BF16)

    for copy in copies[1:]:
        copy.wait()
    q = q_scr[pl.ds(2 * chip, 2), :]
    prod[0:rows, :] = wk[...].astype(F32) * jnp.concatenate([q[0:1], q[1:2]], axis=1)
    fold = lax.dot_general(mine, prod[...], NT, precision=lax.Precision.HIGHEST, preferred_element_type=F32)
    top, mid, low = split3(fold)
    part = jnp.where(sub < 2, top, jnp.where(sub < 4, mid, jnp.where(sub < 6, low, 0.0)))
    w_ref[...] = jnp.concatenate([wv[...].astype(F32), part], axis=0).astype(BF16)


def table_kernel(pw_ref, ve_ref, gain_ref, bias_ref, hi_ref, lo_ref, gram_ref, ac, af):
    n_pw, width = pw_ref.shape
    n_ve = ve_ref.shape[0]
    total = af.shape[0]
    at = n_pw + 4
    gain = gain_ref[...]

    def centered(x):
        return x - jnp.mean(x, axis=-1, keepdims=True)

    pw = centered(pw_ref[...].astype(F32))
    tiles = width // 128
    for i in range(tiles):
        ac[i, 0:n_pw, :] = pw[:, 128 * i : 128 * i + 128]
    af[0:n_pw, :] = pw * gain
    af[n_pw:at, :] = jnp.zeros((at - n_pw, width), F32)
    ve = centered(ve_ref[...].astype(F32))
    af[at : at + n_ve, :] = ve * gain
    af[at + n_ve : at + n_ve + 1, :] = bias_ref[...]
    af[at + n_ve + 1 : total, :] = jnp.zeros((total - at - n_ve - 1, width), F32)
    a = af[...]
    hi = a.astype(BF16)
    hi_ref[...] = hi
    lo_ref[...] = (a - hi.astype(F32)).astype(BF16)

    sums = [jnp.zeros((n_ve, 128), F32) for _ in PAIRS]
    for i in range(tiles):
        planes = [ac[i, pl.ds(k, n_ve, stride=4), :] for k in range(4)] + [ve[:, 128 * i : 128 * i + 128]]
        sums = [total + planes[k] * planes[l] for total, (k, l) in zip(sums, PAIRS, strict=True)]
    lane = iota((n_ve, 128), 1)
    gram = jnp.zeros((n_ve, 128), F32)
    for i, (k, l) in enumerate(PAIRS):
        g = jnp.sum(sums[i], axis=-1, keepdims=True) * ((1.0 if k == l else 2.0) / width)
        gram = jnp.where(lane == i, g, gram)
    top, mid, low = split3(gram)
    gram = top + pltpu.roll(mid, 16, 1) + pltpu.roll(low, 32, 1)
    gram_ref[...] = jnp.zeros(gram_ref.shape, BF16)
    gram_ref[0:n_ve, :] = gram.astype(BF16)


def attend_kernel(core_ref, count_ref, hi_ref, lo_ref, gram_ref, both_ref, out_ref, wv_scr, f_scr, w_scr, v_scr):
    half = core_ref[0]
    count = count_ref[0]
    n_dp = both_ref.shape[1]
    rows = both_ref.shape[2] - 8
    per = 128 // rows
    for d in range(n_dp):
        wv_scr[d * rows : (d + 1) * rows, :] = both_ref[0, d, 0:rows, :]
    for i in range(n_dp // per):
        tile = jnp.zeros((8, 128), F32)
        for p in range(per):
            piece = both_ref[0, i * per + p, rows : rows + 8, :].astype(F32)
            tile = tile + (pltpu.roll(piece, rows * p, 1) if p else piece)
        f_scr[:, 128 * i : 128 * i + 128] = tile.astype(BF16)
    hi, lo = hi_ref[...], lo_ref[...]
    wv, f = wv_scr[...], f_scr[...]
    t = jnp.dot(hi, wv, preferred_element_type=F32) + jnp.dot(lo, wv, preferred_element_type=F32)
    thi = t.astype(BF16)
    tlo = (t - thi.astype(F32)).astype(BF16)
    keys = lax.dot_general(f, hi, NT, preferred_element_type=F32)
    keys = keys + lax.dot_general(f, lo, NT, preferred_element_type=F32)
    keys = (keys + pltpu.roll(keys, 6, 0) + pltpu.roll(keys, 4, 0)) * 0.125
    key_row = jnp.where(half == 0, keys[0:1], keys[1:2])

    slots = w_scr.shape[0] // 5
    entries = hi_ref.shape[0]
    n_ve = gram_ref.shape[0]
    at = entries - n_ve
    n_sv = slots // 6
    x = both_ref[1].reshape(n_dp * (rows + 8), 128)[0 : 64 * n_sv, :].reshape(n_sv, 2, 32, 128)
    x = jnp.concatenate([x[:, i].reshape(32 * n_sv, 128) for i in range(2)], axis=1)
    n_rows = x.shape[0]
    n = iota((slots, n_rows), 0)
    group = (n * 43) >> 8
    base = group * 32
    within = n - group * 6
    col = iota((slots, n_rows), 1)

    def picked(hit):
        return jnp.where(hit, 1.0, 0.0).astype(BF16)

    meta = jnp.dot(picked(col == base + 24 + within), x[:, :128], preferred_element_type=F32)
    c = [jnp.dot(picked(col == base + within * 4 + k), x, preferred_element_type=F32) for k in range(4)]
    ids = meta[:, 0:1].astype(jnp.int32)
    gram = jnp.dot(picked(iota((slots, n_ve), 1) == ids), gram_ref[...], preferred_element_type=F32)
    gram = gram + pltpu.roll(gram, 112, 1) + pltpu.roll(gram, 96, 1)

    col = iota((slots, entries), 1)
    is_value = iota((slots, 128), 1) // 64 == half
    keyed = []
    for k in range(5):
        hit = col == (4 * ids + k if k < 4 else at + ids)
        keyed.append(jnp.sum(jnp.where(hit, key_row, 0.0), axis=1, keepdims=True))
        v = jnp.dot(picked(hit), thi, preferred_element_type=F32)
        v_scr[k * slots : (k + 1) * slots, :] = jnp.where(is_value, v, 0.0).astype(BF16)
    bias_row = t[at + 91 : at + 92, :]
    key_bias = key_row[:, at + 91 : at + 92]
    value_bias = jnp.where(is_value[0:1, :], bias_row, 0.0)

    def g(k, l):
        i = PAIRS.index((k, l))
        return gram[:, i : i + 1]

    spread = g(4, 4)
    for k in range(4):
        inner = g(k, 4)
        for l in range(k, 4):
            inner = inner + g(k, l) * c[l]
        spread = spread + c[k] * inner
    r = lax.rsqrt(jnp.maximum(spread, 0.0) + 1e-05)
    dots = keyed[4]
    for k in range(4):
        dots = dots + c[k] * keyed[k]
    scores = r * dots + key_bias
    scores = jnp.where(iota(scores.shape, 0) < count, scores, -1e30)
    peak = jnp.max(scores, axis=0, keepdims=True)
    expo = jnp.exp(scores - peak)
    share = expo * (1.0 / jnp.sum(expo, axis=0, keepdims=True)) * r
    for k in range(4):
        w_scr[k * slots : (k + 1) * slots, :] = (share * c[k]).astype(BF16)
    w_scr[4 * slots :, :] = share.astype(BF16)
    mixed = lax.dot_general(w_scr[...], v_scr[...], TN, preferred_element_type=F32)
    out_ref[...] = (mixed + value_bias).astype(BF16)


def project_out_kernel(m_ref, wo_ref, out_ref):
    parts = [m_ref[2 * i].astype(F32) + m_ref[2 * i + 1].astype(F32) for i in range(m_ref.shape[0] // 2)]
    mixed = jnp.concatenate(parts, axis=1).astype(BF16)
    out_ref[...] = jnp.dot(mixed, wo_ref[...], preferred_element_type=F32).astype(BF16)


def cost(flops, moved):
    return pl.CostEstimate(flops=flops, transcendentals=0, bytes_accessed=moved)


def on_device(
    pixels,
    var_ids,
    counts,
    patch_weight,
    var_embed,
    norm_gain,
    norm_bias,
    key_weight,
    value_weight,
    query,
    out_weight,
):
    slots, pp, patches = pixels.shape[1:]
    n_var, width = var_embed.shape
    n_dp = lax.axis_size(DP)
    n_chip, n_core = lax.axis_size("y"), lax.axis_size("core")
    n_sv = n_chip * n_core
    all_slots = slots * n_sv
    entries = 464
    rows = key_weight.shape[0] + 8
    smem, vmem = whole(pltpu.SMEM), whole()
    chip = lax.axis_index("y").astype(jnp.int32).reshape(1)
    core = lax.axis_index("core").astype(jnp.int32).reshape(1)

    packed_w, packed_x = pl.pallas_call(
        pack_kernel,
        out_shape=(jax.ShapeDtypeStruct((rows, 128), BF16), jax.ShapeDtypeStruct((64, 128), BF16)),
        in_specs=[smem, smem] + [whole(pltpu.HBM)] * 4,
        out_specs=(vmem, vmem),
        scratch_shapes=[
            pltpu.VMEM((rows - 8, 128), BF16),
            pltpu.VMEM((rows - 8, 128), BF16),
            pltpu.VMEM(query.shape, F32),
            pltpu.VMEM(pixels.shape, BF16),
            pltpu.VMEM((128, 128), F32),
            pltpu.VMEM((64, 128), F32),
            pltpu.SemaphoreType.DMA((4,)),
        ],
        name="pack",
    )(chip, var_ids, key_weight, value_weight, query, pixels)
    of_chip = lax.all_gather(packed_x, "core")

    def tables(patch_weight, var_embed, norm_gain, norm_bias):
        return pl.pallas_call(
            table_kernel,
            out_shape=(
                jax.ShapeDtypeStruct((entries, width), BF16),
                jax.ShapeDtypeStruct((entries, width), BF16),
                jax.ShapeDtypeStruct((96, 128), BF16),
            ),
            in_specs=[vmem] * 4,
            out_specs=(vmem,) * 3,
            scratch_shapes=[pltpu.VMEM((width // 128, n_var * pp + 4, 128), F32), pltpu.VMEM((entries, width), F32)],
            cost_estimate=cost(20 * entries * width, 8 * entries * width),
            compiler_params=pltpu.CompilerParams(vmem_limit_bytes=24 << 20),
            name="tables",
        )(
            patch_weight.reshape(n_var * pp, width),
            var_embed,
            norm_gain.reshape(1, width),
            norm_bias.reshape(1, width),
        )

    def weights_of_all(packed_w, of_chip, *params):
        send = jnp.broadcast_to(packed_w, (n_dp, *packed_w.shape))
        return lax.all_to_all(send, DP, 0, 0, tiled=True), *tables(*params)

    def pixels_of_all(packed_w, of_chip, *params):
        send = jnp.broadcast_to(of_chip, (n_chip, *of_chip.shape))
        got = lax.all_to_all(send, "y", 0, 0, tiled=True).reshape(-1, 128)
        got = jnp.pad(got, ((0, n_dp * rows - got.shape[0]), (0, 0))).reshape(n_dp, rows, 128)
        return got, *tables(*params)

    params = (patch_weight, var_embed, norm_gain, norm_bias)
    mine, hi, lo, gram = lax.cond(core[0] == 0, weights_of_all, pixels_of_all, packed_w, of_chip, *params)
    both = lax.all_gather(mine, "core")

    mixed = pl.pallas_call(
        attend_kernel,
        out_shape=jax.ShapeDtypeStruct((patches, 128), BF16),
        in_specs=[smem, smem] + [vmem] * 4,
        out_specs=vmem,
        scratch_shapes=[
            pltpu.VMEM((width, 128), BF16),
            pltpu.VMEM((8, width), BF16),
            pltpu.VMEM((5 * all_slots, patches), BF16),
            pltpu.VMEM((5 * all_slots, 128), BF16),
        ],
        compiler_params=pltpu.CompilerParams(vmem_limit_bytes=24 << 20),
        name="attend",
    )(core, counts, hi, lo, gram, both)
    owned = lax.all_to_all(mixed.reshape(n_sv, patches // n_sv, 128), VAR, 0, 0, tiled=True)

    out = pl.pallas_call(
        project_out_kernel,
        out_shape=jax.ShapeDtypeStruct((patches // n_sv, width), BF16),
        in_specs=[vmem, vmem],
        out_specs=vmem,
        compiler_params=pltpu.CompilerParams(vmem_limit_bytes=16 << 20),
        name="project_out",
    )(owned, out_weight)
    return out[None]


def solution(mesh):
    torus = Mesh(mesh.devices.reshape(4, 8, 8, 2), (*DP, *VAR))
    return jax.shard_map(
        on_device,
        mesh=torus,
        in_specs=(
            P(DP, VAR, None, None),
            P(DP, VAR),
            P(DP),
            P(),
            P(),
            P(),
            P(),
            P(DP, None),
            P(DP, None),
            P(),
            P(),
        ),
        out_specs=P(DP, VAR, None),
        check_vma=False,
    )
```

```python
import jax
import jax.numpy as jnp
from jax import lax
from jax.experimental import pallas as pl
from jax.experimental.pallas import tpu as pltpu
from jax.sharding import Mesh
from jax.sharding import PartitionSpec as P

DP = ("dp_0", "dp_1")
VAR = ("y", "core")
F32 = jnp.float32
BF16 = jnp.bfloat16
NT = (((1,), (1,)), ((), ()))
TN = (((0,), (0,)), ((), ()))
PAIRS = [(k, l) for k in range(5) for l in range(k, 5)]


def whole(memory_space=pltpu.VMEM):
    return pl.BlockSpec(memory_space=memory_space)


def iota(shape, dim):
    return lax.broadcasted_iota(jnp.int32, shape, dim)


def picked(hits):
    return jnp.concatenate([jnp.where(hit, 1.0, 0.0) for hit in hits], axis=0).astype(BF16)


def split3(x):
    top = x.astype(BF16).astype(F32)
    mid = (x - top).astype(BF16).astype(F32)
    return top, mid, (x - top - mid).astype(BF16).astype(F32)


def pack_kernel(chip_ref, ids_ref, wk_ref, wv_ref, query_ref, pix_ref, w_ref, send_ref, wk, wv, q_scr, pix, ids, prod, chunk, sems):
    chip = chip_ref[0]
    at = pl.multiple_of(chip * 128, 128)
    copies = [
        pltpu.make_async_copy(ids_ref, ids, sems.at[0]),
        pltpu.make_async_copy(pix_ref, pix, sems.at[1]),
        pltpu.make_async_copy(query_ref, q_scr, sems.at[2]),
        pltpu.make_async_copy(wk_ref.at[:, pl.ds(at, 128)], wk, sems.at[3]),
        pltpu.make_async_copy(wv_ref.at[:, pl.ds(at, 128)], wv, sems.at[4]),
    ]
    for copy in copies:
        copy.start()
    rows = wk.shape[0]
    slots = ids_ref.shape[1]
    prod[...] = jnp.zeros(prod.shape, F32)
    sub, lane = iota((8, 128), 0), iota((8, 128), 1)
    mine = jnp.where(lane // 64 == sub % 2, 1.0, 0.0).astype(BF16)
    for copy in copies[:2]:
        copy.wait()
    own = iota((8, slots), 0) == iota((8, slots), 1)
    meta = jnp.sum(jnp.where(own, ids[...].astype(F32), 0.0), axis=1, keepdims=True)
    meta = jnp.broadcast_to(meta, (8, 128))
    n = 4 * slots
    for half in range(2):
        chunk[32 * half + n : 32 * half + 32, :] = meta
    for s in range(slots):
        x = pix[0, s].astype(F32)
        for half in range(2):
            chunk[32 * half + 4 * s : 32 * half + 4 * s + 4, :] = x[:, 128 * half : 128 * half + 128]
    send_ref[...] = chunk[...].astype(BF16)

    for copy in copies[2:]:
        copy.wait()
    q = q_scr[pl.ds(2 * chip, 2), :]
    prod[0:rows, :] = wk[...].astype(F32) * jnp.concatenate([q[0:1], q[1:2]], axis=1)
    parts = [lax.dot_general(mine, part.astype(BF16), NT, preferred_element_type=F32) for part in split3(prod[...])]
    fold = parts[0] + parts[1] + parts[2]
    top, mid, low = split3(fold)
    part = jnp.where(sub < 2, top, jnp.where(sub < 4, mid, jnp.where(sub < 6, low, 0.0)))
    both = jnp.concatenate([wv[...].astype(F32), part], axis=0).astype(BF16)
    for d in range(w_ref.shape[0]):
        w_ref[d] = both


def table_kernel(pw_ref, ve_ref, gain_ref, bias_ref, hi_ref, lo_ref, gram_ref, ac, af):
    n_pw, width = pw_ref.shape
    n_ve = ve_ref.shape[0]
    total = af.shape[0]
    at = n_pw + 4
    gain = gain_ref[...]

    def centered(x):
        return x - jnp.mean(x, axis=-1, keepdims=True)

    pw = centered(pw_ref[...].astype(F32))
    tiles = width // 128
    for i in range(tiles):
        ac[i, 0:n_pw, :] = pw[:, 128 * i : 128 * i + 128]
    af[0:n_pw, :] = pw * gain
    af[n_pw:at, :] = jnp.zeros((at - n_pw, width), F32)
    ve = centered(ve_ref[...].astype(F32))
    af[at : at + n_ve, :] = ve * gain
    af[at + n_ve : at + n_ve + 1, :] = bias_ref[...]
    af[at + n_ve + 1 : total, :] = jnp.zeros((total - at - n_ve - 1, width), F32)
    a = af[...]
    hi = a.astype(BF16)
    hi_ref[...] = hi
    lo_ref[...] = (a - hi.astype(F32)).astype(BF16)

    sums = [jnp.zeros((n_ve, 128), F32) for _ in PAIRS]
    for i in range(tiles):
        planes = [ac[i, pl.ds(k, n_ve, stride=4), :] for k in range(4)] + [ve[:, 128 * i : 128 * i + 128]]
        sums = [total + planes[k] * planes[l] for total, (k, l) in zip(sums, PAIRS, strict=True)]
    lane = iota((n_ve, 128), 1)
    gram = jnp.zeros((n_ve, 128), F32)
    for i, (k, l) in enumerate(PAIRS):
        g = jnp.sum(sums[i], axis=-1, keepdims=True) * ((1.0 if k == l else 2.0) / width)
        gram = jnp.where(lane == i, g, gram)
    top, mid, low = split3(gram)
    gram = top + pltpu.roll(mid, 16, 1) + pltpu.roll(low, 32, 1)
    gram_ref[...] = jnp.zeros(gram_ref.shape, BF16)
    gram_ref[0:n_ve, :] = gram.astype(BF16)


def slots_kernel(count_ref, got_ref, gram_ref, out_ref):
    n_chip = got_ref.shape[0]
    slots = 12 * n_chip
    x = got_ref[...].reshape(2 * n_chip, 2, 32, 128)
    x = jnp.concatenate([x[:, i].reshape(64 * n_chip, 128) for i in range(2)], axis=1)
    n = iota((slots, x.shape[0]), 0)
    group = (n * 43) >> 8
    within = n - group * 6
    col = iota(n.shape, 1) - group * 32
    hits = [col == within * 4 + k for k in range(4)] + [col == 24 + within]
    moved = jnp.dot(picked(hits), x, preferred_element_type=F32)
    c = [moved[k * slots : (k + 1) * slots] for k in range(4)]
    meta = moved[4 * slots :, :128]
    ids = meta[:, 0:1].astype(jnp.int32)
    n_ve = gram_ref.shape[0]
    gram = jnp.dot(picked([iota((slots, n_ve), 1) == ids]), gram_ref[...], preferred_element_type=F32)
    gram = gram + pltpu.roll(gram, 112, 1) + pltpu.roll(gram, 96, 1)

    def g(k, l):
        i = PAIRS.index((k, l))
        return gram[:, i : i + 1]

    spread = g(4, 4)
    for k in range(4):
        inner = g(k, 4)
        for l in range(k, 4):
            inner = inner + g(k, l) * c[l]
        spread = spread + c[k] * inner
    r = lax.rsqrt(jnp.maximum(spread, 0.0) + 1e-05)
    top = r.astype(BF16)
    planes = [plane.astype(BF16) for plane in c] + [top, (r - top.astype(F32)).astype(BF16)]
    at = 0
    for plane in planes:
        for half in range(2):
            out_ref[at : at + slots, :] = plane[:, 128 * half : 128 * half + 128]
            at += slots
    meta = jnp.where(iota(meta.shape, 1) == 1, count_ref[0].astype(F32), meta)
    out_ref[at : at + slots, :] = meta.astype(BF16)
    at += slots
    out_ref[at:, :] = jnp.zeros((out_ref.shape[0] - at, 128), BF16)


def attend_kernel(core_ref, hi_ref, lo_ref, weights_ref, planes_ref, out_ref, wide, w_scr):
    half = core_ref[0]
    n_dp = weights_ref.shape[1]
    rows = weights_ref.shape[2] - 8
    per = 128 // rows
    for d in range(n_dp):
        wide[d * rows : (d + 1) * rows, 0:128] = weights_ref[0, d, 0:rows, :]
    for i in range(n_dp // per):
        tile = jnp.zeros((8, 128), F32)
        for p in range(per):
            piece = weights_ref[0, i * per + p, rows : rows + 8, :].astype(F32)
            tile = tile + (pltpu.roll(piece, rows * p, 1) if p else piece)
        tile = jnp.concatenate([tile, jnp.zeros((120, 128), F32)], axis=0)
        wide[128 * i : 128 * i + 128, 128:256] = tile.T.astype(BF16)
    w = wide[...]
    t = jnp.dot(hi_ref[...], w, preferred_element_type=F32) + jnp.dot(lo_ref[...], w, preferred_element_type=F32)
    values, keys = t[:, :128], t[:, 128:]
    keys = (keys + pltpu.roll(keys, 126, 1) + pltpu.roll(keys, 124, 1)) * 0.125
    top, mid, low = split3(keys)
    lane = iota(keys.shape, 1)
    parts = jnp.where(lane < 4, pltpu.roll(mid, 2, 1), jnp.where(lane < 6, pltpu.roll(low, 4, 1), 0.0))
    parts = jnp.where(lane < 2, top, parts)
    table = jnp.concatenate([values, parts], axis=1).astype(BF16)

    slots = w_scr.shape[0] // 5
    entries = hi_ref.shape[0]
    at = entries - 96

    def plane(i):
        return jnp.concatenate(
            [planes_ref[1, (2 * i + h) * slots : (2 * i + h + 1) * slots, :].astype(F32) for h in range(2)], axis=1
        )

    meta = planes_ref[1, 12 * slots : 13 * slots, :].astype(F32)
    ids = meta[:, 0:1].astype(jnp.int32)
    col = iota((slots, entries), 1)
    found = jnp.dot(
        picked([col == 4 * ids + k for k in range(4)] + [col == at + ids]), table, preferred_element_type=F32
    )
    lane = iota((5 * slots, 128), 1)
    v = jnp.where(lane // 64 == half, found[:, :128], 0.0).astype(BF16)
    keyed = jnp.sum(jnp.where(lane % 2 == half, found[:, 128:], 0.0), axis=1, keepdims=True)
    one_row = lane[0:1]
    key_bias = jnp.sum(jnp.where(one_row == half, keys[at + 91 : at + 92], 0.0), axis=1, keepdims=True)
    value_bias = jnp.where(one_row // 64 == half, values[at + 91 : at + 92], 0.0)

    c = [plane(k) for k in range(4)]
    r = plane(4) + plane(5)
    dots = keyed[4 * slots :]
    for k in range(4):
        dots = dots + c[k] * keyed[k * slots : (k + 1) * slots]
    scores = r * dots + key_bias
    scores = jnp.where(iota(scores.shape, 0) < meta[:, 1:2].astype(jnp.int32), scores, -1e30)
    peak = jnp.max(scores, axis=0, keepdims=True)
    expo = jnp.exp(scores - peak)
    share = expo * (1.0 / jnp.sum(expo, axis=0, keepdims=True)) * r
    for k in range(4):
        w_scr[k * slots : (k + 1) * slots, :] = (share * c[k]).astype(BF16)
    w_scr[4 * slots :, :] = share.astype(BF16)
    mixed = lax.dot_general(w_scr[...], v, TN, preferred_element_type=F32)
    mixed = mixed + value_bias
    turned = pltpu.roll(mixed, 64, 1)
    first = jnp.where(half == 0, mixed, turned).reshape(-1, 2, 8, 128)
    second = jnp.where(half == 0, turned, mixed).reshape(-1, 2, 8, 128)
    left = iota((first.shape[0], 8, 128), 2) < 64
    out_ref[...] = jnp.where(left, first[:, 0], second[:, 1]).astype(BF16)


def project_out_kernel(m_ref, wo_ref, out_ref):
    left = iota((8, 128), 1) < 64
    parts = []
    for i in range(m_ref.shape[0] // 2):
        a, b = m_ref[2 * i].astype(F32), m_ref[2 * i + 1].astype(F32)
        first = jnp.where(left, a, pltpu.roll(b, 64, 1))
        second = jnp.where(left, pltpu.roll(a, 64, 1), b)
        parts.append(jnp.concatenate([first, second], axis=0))
    mixed = jnp.concatenate(parts, axis=1).astype(BF16)
    out_ref[...] = jnp.dot(mixed, wo_ref[...], preferred_element_type=F32).astype(BF16)


def cost(flops, moved):
    return pl.CostEstimate(flops=flops, transcendentals=0, bytes_accessed=moved)


def on_device(
    pixels,
    var_ids,
    counts,
    patch_weight,
    var_embed,
    norm_gain,
    norm_bias,
    key_weight,
    value_weight,
    query,
    out_weight,
):
    slots, pp, patches = pixels.shape[1:]
    n_var, width = var_embed.shape
    n_dp = lax.axis_size(DP)
    n_chip, n_core = lax.axis_size("y"), lax.axis_size("core")
    n_sv = n_chip * n_core
    all_slots = slots * n_sv
    entries = 464
    rows = key_weight.shape[0] + 8
    smem, vmem = whole(pltpu.SMEM), whole()
    chip = lax.axis_index("y").astype(jnp.int32).reshape(1)
    core = lax.axis_index("core").astype(jnp.int32).reshape(1)

    packed_w, packed_x = pl.pallas_call(
        pack_kernel,
        out_shape=(jax.ShapeDtypeStruct((n_dp, rows, 128), BF16), jax.ShapeDtypeStruct((64, 128), BF16)),
        in_specs=[smem] + [whole(pltpu.HBM)] * 5,
        out_specs=(vmem, vmem),
        scratch_shapes=[
            pltpu.VMEM((rows - 8, 128), BF16),
            pltpu.VMEM((rows - 8, 128), BF16),
            pltpu.VMEM(query.shape, F32),
            pltpu.VMEM(pixels.shape, BF16),
            pltpu.VMEM(var_ids.shape, jnp.int32),
            pltpu.VMEM((128, 128), F32),
            pltpu.VMEM((64, 128), F32),
            pltpu.SemaphoreType.DMA((5,)),
        ],
        name="pack",
    )(chip, var_ids, key_weight, value_weight, query, pixels)
    of_chip = lax.all_gather(packed_x, "core")

    def tables(patch_weight, var_embed, norm_gain, norm_bias):
        return pl.pallas_call(
            table_kernel,
            out_shape=(
                jax.ShapeDtypeStruct((entries, width), BF16),
                jax.ShapeDtypeStruct((entries, width), BF16),
                jax.ShapeDtypeStruct((96, 128), BF16),
            ),
            in_specs=[vmem] * 4,
            out_specs=(vmem,) * 3,
            scratch_shapes=[pltpu.VMEM((width // 128, n_var * pp + 4, 128), F32), pltpu.VMEM((entries, width), F32)],
            cost_estimate=cost(20 * entries * width, 8 * entries * width),
            compiler_params=pltpu.CompilerParams(vmem_limit_bytes=24 << 20),
            name="tables",
        )(
            patch_weight.reshape(n_var * pp, width),
            var_embed,
            norm_gain.reshape(1, width),
            norm_bias.reshape(1, width),
        )

    def weights_of_all(packed_w, of_chip, counts, *params):
        hi, lo, _ = tables(*params)
        return lax.all_to_all(packed_w, DP, 0, 0, tiled=True), hi, lo

    def slots_of_all(packed_w, of_chip, counts, *params):
        hi, lo, gram = tables(*params)
        send = jnp.broadcast_to(of_chip, (n_chip, *of_chip.shape))
        planes = pl.pallas_call(
            slots_kernel,
            out_shape=jax.ShapeDtypeStruct((n_dp * rows, 128), BF16),
            in_specs=[smem, vmem, vmem],
            out_specs=vmem,
            compiler_params=pltpu.CompilerParams(vmem_limit_bytes=24 << 20),
            name="slots",
        )(counts, lax.all_to_all(send, "y", 0, 0, tiled=True), gram)
        return planes.reshape(n_dp, rows, 128), hi, lo

    params = (counts, patch_weight, var_embed, norm_gain, norm_bias)
    mine, hi, lo = lax.cond(core[0] == 0, weights_of_all, slots_of_all, packed_w, of_chip, *params)
    both = lax.all_gather(mine, "core")

    mixed = pl.pallas_call(
        attend_kernel,
        out_shape=jax.ShapeDtypeStruct((n_sv, 8, 128), BF16),
        in_specs=[smem] + [vmem] * 4,
        out_specs=vmem,
        scratch_shapes=[pltpu.VMEM((width, 256), BF16), pltpu.VMEM((5 * all_slots, patches), BF16)],
        compiler_params=pltpu.CompilerParams(vmem_limit_bytes=24 << 20),
        name="attend",
    )(core, hi, lo, both, both.reshape(n_core, n_dp * rows, 128))
    owned = lax.all_to_all(mixed, VAR, 0, 0, tiled=True)

    out = pl.pallas_call(
        project_out_kernel,
        out_shape=jax.ShapeDtypeStruct((patches // n_sv, width), BF16),
        in_specs=[vmem, vmem],
        out_specs=vmem,
        compiler_params=pltpu.CompilerParams(vmem_limit_bytes=16 << 20),
        name="project_out",
    )(owned, out_weight)
    return out[None]


def solution(mesh):
    torus = Mesh(mesh.devices.reshape(4, 8, 8, 2), (*DP, *VAR))
    return jax.shard_map(
        on_device,
        mesh=torus,
        in_specs=(
            P(DP, VAR, None, None),
            P(DP, VAR),
            P(DP),
            P(),
            P(),
            P(),
            P(),
            P(DP, None),
            P(DP, None),
            P(),
            P(),
        ),
        out_specs=P(DP, VAR, None),
        check_vma=False,
    )
```

```python
import jax
import jax.numpy as jnp
from jax import lax
from jax.experimental import pallas as pl
from jax.experimental.pallas import tpu as pltpu
from jax.sharding import Mesh
from jax.sharding import PartitionSpec as P

DP = ("dp_0", "dp_1")
VAR = ("y", "core")
F32 = jnp.float32
BF16 = jnp.bfloat16
NT = (((1,), (1,)), ((), ()))
TN = (((0,), (0,)), ((), ()))
PAIRS = [(k, l) for k in range(5) for l in range(k, 5)]


def whole(memory_space=pltpu.VMEM):
    return pl.BlockSpec(memory_space=memory_space)


def iota(shape, dim):
    return lax.broadcasted_iota(jnp.int32, shape, dim)


def picked(hits):
    return jnp.concatenate([jnp.where(hit, 1.0, 0.0) for hit in hits], axis=0).astype(BF16)


def split3(x):
    top = x.astype(BF16).astype(F32)
    mid = (x - top).astype(BF16).astype(F32)
    return top, mid, (x - top - mid).astype(BF16).astype(F32)


def pack_kernel(ids_ref, wk_ref, wv_ref, query_ref, pix_ref, w_ref, send_ref, wk, wv, q_scr, pix, ids, prod, chunk, sems):
    chip = lax.axis_index("y")
    at = pl.multiple_of(chip * 128, 128)
    copies = [
        pltpu.make_async_copy(ids_ref, ids, sems.at[0]),
        pltpu.make_async_copy(pix_ref, pix, sems.at[1]),
        pltpu.make_async_copy(query_ref, q_scr, sems.at[2]),
        pltpu.make_async_copy(wk_ref.at[:, pl.ds(at, 128)], wk, sems.at[3]),
        pltpu.make_async_copy(wv_ref.at[:, pl.ds(at, 128)], wv, sems.at[4]),
    ]
    for copy in copies:
        copy.start()
    rows = wk.shape[0]
    slots = ids_ref.shape[1]
    prod[...] = jnp.zeros(prod.shape, F32)
    sub, lane = iota((8, 128), 0), iota((8, 128), 1)
    mine = jnp.where(lane // 64 == sub % 2, 1.0, 0.0).astype(BF16)
    for copy in copies[:2]:
        copy.wait()
    own = iota((8, slots), 0) == iota((8, slots), 1)
    meta = jnp.sum(jnp.where(own, ids[...].astype(F32), 0.0), axis=1, keepdims=True)
    meta = jnp.broadcast_to(meta, (8, 128))
    n = 4 * slots
    for half in range(2):
        chunk[32 * half + n : 32 * half + 32, :] = meta
    for s in range(slots):
        x = pix[0, s].astype(F32)
        for half in range(2):
            chunk[32 * half + 4 * s : 32 * half + 4 * s + 4, :] = x[:, 128 * half : 128 * half + 128]
    send_ref[...] = chunk[...].astype(BF16)

    for copy in copies[2:]:
        copy.wait()
    q = q_scr[pl.ds(2 * chip, 2), :]
    prod[0:rows, :] = wk[...].astype(F32) * jnp.concatenate([q[0:1], q[1:2]], axis=1)
    parts = [lax.dot_general(mine, part.astype(BF16), NT, preferred_element_type=F32) for part in split3(prod[...])]
    fold = parts[0] + parts[1] + parts[2]
    top, mid, low = split3(fold)
    part = jnp.where(sub < 2, top, jnp.where(sub < 4, mid, jnp.where(sub < 6, low, 0.0)))
    both = jnp.concatenate([wv[...].astype(F32), part], axis=0).astype(BF16)
    for d in range(w_ref.shape[0]):
        w_ref[d] = both


def table_kernel(pw_ref, ve_ref, gain_ref, bias_ref, rows_ref, gram_ref, ac):
    n_pw, width = pw_ref.shape
    n_ve = ve_ref.shape[0]
    total = rows_ref.shape[0]
    at = n_pw + 4
    gain = gain_ref[...]

    def centered(x):
        return x - jnp.mean(x, axis=-1, keepdims=True)

    pw = centered(pw_ref[...].astype(F32))
    tiles = width // 128
    for i in range(tiles):
        ac[i, 0:n_pw, :] = pw[:, 128 * i : 128 * i + 128]
    ve = centered(ve_ref[...].astype(F32))
    pw = jnp.concatenate([pw * gain, jnp.zeros((at - n_pw, width), F32)], axis=0)
    rows_ref[0:at, :] = pw.astype(BF16)
    rest = jnp.zeros((total - at - n_ve - 1, width), F32)
    rows_ref[at:, :] = jnp.concatenate([ve * gain, bias_ref[...], rest], axis=0).astype(BF16)

    sums = [jnp.zeros((n_ve, 128), F32) for _ in PAIRS]
    for i in range(tiles):
        planes = [ac[i, pl.ds(k, n_ve, stride=4), :] for k in range(4)] + [ve[:, 128 * i : 128 * i + 128]]
        sums = [total + planes[k] * planes[l] for total, (k, l) in zip(sums, PAIRS, strict=True)]
    lane = iota((n_ve, 128), 1)
    gram = jnp.zeros((n_ve, 128), F32)
    for i, (k, l) in enumerate(PAIRS):
        g = jnp.sum(sums[i], axis=-1, keepdims=True) * ((1.0 if k == l else 2.0) / width)
        gram = jnp.where(lane == i, g, gram)
    top, mid, low = split3(gram)
    gram = top + pltpu.roll(mid, 16, 1) + pltpu.roll(low, 32, 1)
    gram_ref[...] = jnp.zeros(gram_ref.shape, BF16)
    gram_ref[0:n_ve, :] = gram.astype(BF16)


def slots_kernel(count_ref, got_ref, gram_ref, out_ref):
    n_chip = got_ref.shape[0]
    slots = 12 * n_chip
    x = got_ref[...].reshape(2 * n_chip, 2, 32, 128)
    x = jnp.concatenate([x[:, i].reshape(64 * n_chip, 128) for i in range(2)], axis=1)
    n = iota((slots, x.shape[0]), 0)
    group = (n * 43) >> 8
    within = n - group * 6
    col = iota(n.shape, 1) - group * 32
    hits = [col == within * 4 + k for k in range(4)] + [col == 24 + within]
    moved = jnp.dot(picked(hits), x, preferred_element_type=F32)
    c = [moved[k * slots : (k + 1) * slots] for k in range(4)]
    meta = moved[4 * slots :, :128]
    ids = meta[:, 0:1].astype(jnp.int32)
    n_ve = gram_ref.shape[0]
    gram = jnp.dot(picked([iota((slots, n_ve), 1) == ids]), gram_ref[...], preferred_element_type=F32)
    gram = gram + pltpu.roll(gram, 112, 1) + pltpu.roll(gram, 96, 1)

    def g(k, l):
        i = PAIRS.index((k, l))
        return gram[:, i : i + 1]

    spread = g(4, 4)
    for k in range(4):
        inner = g(k, 4)
        for l in range(k, 4):
            inner = inner + g(k, l) * c[l]
        spread = spread + c[k] * inner
    r = lax.rsqrt(jnp.maximum(spread, 0.0) + 1e-05)
    top = r.astype(BF16)
    planes = [plane.astype(BF16) for plane in c] + [top, (r - top.astype(F32)).astype(BF16)]
    at = 0
    for plane in planes:
        for half in range(2):
            out_ref[at : at + slots, :] = plane[:, 128 * half : 128 * half + 128]
            at += slots
    meta = jnp.where(iota(meta.shape, 1) == 1, count_ref[0].astype(F32), meta)
    out_ref[at : at + slots, :] = meta.astype(BF16)
    at += slots
    out_ref[at:, :] = jnp.zeros((out_ref.shape[0] - at, 128), BF16)


def attend_kernel(rows_ref, weights_ref, planes_ref, out_ref, wide, w_scr):
    half = lax.axis_index("core")
    n_dp = weights_ref.shape[1]
    rows = weights_ref.shape[2] - 8
    per = 128 // rows
    for d in range(n_dp):
        wide[d * rows : (d + 1) * rows, 0:128] = weights_ref[0, d, 0:rows, :]
    for i in range(n_dp // per):
        tile = jnp.zeros((8, 128), F32)
        for p in range(per):
            piece = weights_ref[0, i * per + p, rows : rows + 8, :].astype(F32)
            tile = tile + (pltpu.roll(piece, rows * p, 1) if p else piece)
        tile = jnp.concatenate([tile, jnp.zeros((120, 128), F32)], axis=0)
        wide[128 * i : 128 * i + 128, 128:256] = tile.T.astype(BF16)
    w = wide[...]
    t = jnp.dot(rows_ref[...], w, preferred_element_type=F32)
    values, keys = t[:, :128], t[:, 128:]
    top, mid, low = split3(keys)
    parts = top + pltpu.roll(mid, 8, 1) + pltpu.roll(low, 16, 1)
    table = jnp.concatenate([values, parts], axis=1).astype(BF16)

    slots = w_scr.shape[0] // 5
    entries = rows_ref.shape[0]
    at = entries - 96

    def plane(i):
        return jnp.concatenate(
            [planes_ref[1, (2 * i + h) * slots : (2 * i + h + 1) * slots, :].astype(F32) for h in range(2)], axis=1
        )

    meta = planes_ref[1, 12 * slots : 13 * slots, :].astype(F32)
    ids = meta[:, 0:1].astype(jnp.int32)
    col = iota((slots, entries), 1)
    found = jnp.dot(
        picked([col == 4 * ids + k for k in range(4)] + [col == at + ids]), table, preferred_element_type=F32
    )
    lane = iota((1, 128), 1)
    key_lanes = jnp.where(lane % 2 == half, 0.125, 0.0)
    value_lanes = jnp.where(lane // 64 == half, 1.0, 0.0)
    v = (found[:, :128] * value_lanes).astype(BF16)
    keyed = jnp.sum(found[:, 128:] * key_lanes, axis=1, keepdims=True)
    key_bias = jnp.sum(keys[at + 91 : at + 92] * key_lanes, axis=1, keepdims=True)
    value_bias = values[at + 91 : at + 92] * value_lanes

    c = [plane(k) for k in range(4)]
    r = plane(4) + plane(5)
    dots = keyed[4 * slots :]
    for k in range(4):
        dots = dots + c[k] * keyed[k * slots : (k + 1) * slots]
    scores = r * dots + key_bias
    scores = jnp.where(iota(scores.shape, 0) < meta[:, 1:2].astype(jnp.int32), scores, -1e30)
    peak = jnp.max(scores, axis=0, keepdims=True)
    expo = jnp.exp(scores - peak)
    share = expo * (1.0 / jnp.sum(expo, axis=0, keepdims=True)) * r
    for k in range(4):
        w_scr[k * slots : (k + 1) * slots, :] = (share * c[k]).astype(BF16)
    w_scr[4 * slots :, :] = share.astype(BF16)
    mixed = lax.dot_general(v, w_scr[...], TN, preferred_element_type=F32).T
    mixed = mixed + value_bias
    turned = pltpu.roll(mixed, 64, 1)
    first = jnp.where(half == 0, mixed, turned).reshape(-1, 2, 8, 128)
    second = jnp.where(half == 0, turned, mixed).reshape(-1, 2, 8, 128)
    left = iota((first.shape[0], 8, 128), 2) < 64
    out_ref[...] = jnp.where(left, first[:, 0], second[:, 1]).astype(BF16)


def project_out_kernel(m_ref, wo_ref, out_ref):
    left = iota((8, 128), 1) < 64
    parts = []
    for i in range(m_ref.shape[0] // 2):
        a, b = m_ref[2 * i].astype(F32), m_ref[2 * i + 1].astype(F32)
        first = jnp.where(left, a, pltpu.roll(b, 64, 1))
        second = jnp.where(left, pltpu.roll(a, 64, 1), b)
        parts.append(jnp.concatenate([first, second], axis=0))
    mixed = jnp.concatenate(parts, axis=1).astype(BF16)
    out_ref[...] = jnp.dot(mixed, wo_ref[...], preferred_element_type=F32).astype(BF16)


def cost(flops, moved):
    return pl.CostEstimate(flops=flops, transcendentals=0, bytes_accessed=moved)


def on_device(
    pixels,
    var_ids,
    counts,
    patch_weight,
    var_embed,
    norm_gain,
    norm_bias,
    key_weight,
    value_weight,
    query,
    out_weight,
):
    slots, pp, patches = pixels.shape[1:]
    n_var, width = var_embed.shape
    n_dp = lax.axis_size(DP)
    n_chip, n_core = lax.axis_size("y"), lax.axis_size("core")
    n_sv = n_chip * n_core
    all_slots = slots * n_sv
    entries = 464
    rows = key_weight.shape[0] + 8
    smem, vmem = whole(pltpu.SMEM), whole()

    packed_w, packed_x = pl.pallas_call(
        pack_kernel,
        out_shape=(jax.ShapeDtypeStruct((n_dp, rows, 128), BF16), jax.ShapeDtypeStruct((64, 128), BF16)),
        in_specs=[whole(pltpu.HBM)] * 5,
        out_specs=(vmem, vmem),
        scratch_shapes=[
            pltpu.VMEM((rows - 8, 128), BF16),
            pltpu.VMEM((rows - 8, 128), BF16),
            pltpu.VMEM(query.shape, F32),
            pltpu.VMEM(pixels.shape, BF16),
            pltpu.VMEM(var_ids.shape, jnp.int32),
            pltpu.VMEM((128, 128), F32),
            pltpu.VMEM((64, 128), F32),
            pltpu.SemaphoreType.DMA((5,)),
        ],
        name="pack",
    )(var_ids, key_weight, value_weight, query, pixels)
    of_chip = lax.all_gather(packed_x, "core")

    def tables(patch_weight, var_embed, norm_gain, norm_bias):
        return pl.pallas_call(
            table_kernel,
            out_shape=(
                jax.ShapeDtypeStruct((entries, width), BF16),
                jax.ShapeDtypeStruct((96, 128), BF16),
            ),
            in_specs=[vmem] * 4,
            out_specs=(vmem,) * 2,
            scratch_shapes=[pltpu.VMEM((width // 128, n_var * pp + 4, 128), F32)],
            cost_estimate=cost(20 * entries * width, 8 * entries * width),
            compiler_params=pltpu.CompilerParams(vmem_limit_bytes=24 << 20),
            name="tables",
        )(
            patch_weight.reshape(n_var * pp, width),
            var_embed,
            norm_gain.reshape(1, width),
            norm_bias.reshape(1, width),
        )

    def weights_of_all(packed_w, of_chip, counts, *params):
        table, _ = tables(*params)
        return lax.all_to_all(packed_w, DP, 0, 0, tiled=True), table

    def slots_of_all(packed_w, of_chip, counts, *params):
        table, gram = tables(*params)
        send = jnp.broadcast_to(of_chip, (n_chip, *of_chip.shape))
        planes = pl.pallas_call(
            slots_kernel,
            out_shape=jax.ShapeDtypeStruct((n_dp * rows, 128), BF16),
            in_specs=[smem, vmem, vmem],
            out_specs=vmem,
            compiler_params=pltpu.CompilerParams(vmem_limit_bytes=24 << 20),
            name="slots",
        )(counts, lax.all_to_all(send, "y", 0, 0, tiled=True), gram)
        return planes.reshape(n_dp, rows, 128), table

    params = (counts, patch_weight, var_embed, norm_gain, norm_bias)
    mine, table = lax.cond(lax.axis_index("core") == 0, weights_of_all, slots_of_all, packed_w, of_chip, *params)
    both = lax.all_gather(mine, "core")

    mixed = pl.pallas_call(
        attend_kernel,
        out_shape=jax.ShapeDtypeStruct((n_sv, 8, 128), BF16),
        in_specs=[vmem] * 3,
        out_specs=vmem,
        scratch_shapes=[pltpu.VMEM((width, 256), BF16), pltpu.VMEM((5 * all_slots, patches), BF16)],
        compiler_params=pltpu.CompilerParams(vmem_limit_bytes=24 << 20),
        name="attend",
    )(table, both, both.reshape(n_core, n_dp * rows, 128))
    owned = lax.all_to_all(mixed, VAR, 0, 0, tiled=True)

    out = pl.pallas_call(
        project_out_kernel,
        out_shape=jax.ShapeDtypeStruct((patches // n_sv, width), BF16),
        in_specs=[vmem, vmem],
        out_specs=vmem,
        compiler_params=pltpu.CompilerParams(vmem_limit_bytes=16 << 20),
        name="project_out",
    )(owned, out_weight)
    return out[None]


def solution(mesh):
    torus = Mesh(mesh.devices.reshape(4, 8, 8, 2), (*DP, *VAR))
    return jax.shard_map(
        on_device,
        mesh=torus,
        in_specs=(
            P(DP, VAR, None, None),
            P(DP, VAR),
            P(DP),
            P(),
            P(),
            P(),
            P(),
            P(DP, None),
            P(DP, None),
            P(),
            P(),
        ),
        out_specs=P(DP, VAR, None),
        check_vma=False,
    )
```

```python
import jax
import jax.numpy as jnp
from jax import lax
from jax.experimental import pallas as pl
from jax.experimental.pallas import tpu as pltpu
from jax.sharding import Mesh
from jax.sharding import PartitionSpec as P

DP = ("dp_0", "dp_1")
VAR = ("y", "core")
F32 = jnp.float32
BF16 = jnp.bfloat16
NT = (((1,), (1,)), ((), ()))
TN = (((0,), (0,)), ((), ()))
PAIRS = [(k, l) for k in range(5) for l in range(k, 5)]


def whole(memory_space=pltpu.VMEM):
    return pl.BlockSpec(memory_space=memory_space)


def iota(shape, dim):
    return lax.broadcasted_iota(jnp.int32, shape, dim)


def picked(hits):
    return jnp.concatenate([jnp.where(hit, 1.0, 0.0) for hit in hits], axis=0).astype(BF16)


def split3(x):
    top = x.astype(BF16).astype(F32)
    mid = (x - top).astype(BF16).astype(F32)
    return top, mid, (x - top - mid).astype(BF16).astype(F32)


def pack_kernel(ids_ref, wk_ref, wv_ref, query_ref, pix_ref, w_ref, send_ref, wk, wv, q_scr, pix, ids, prod, chunk, stage, sems):
    chip = lax.axis_index("y")
    at = pl.multiple_of(chip * 128, 128)
    copies = [
        pltpu.make_async_copy(ids_ref, ids, sems.at[0]),
        pltpu.make_async_copy(pix_ref, pix, sems.at[1]),
        pltpu.make_async_copy(query_ref, q_scr, sems.at[2]),
        pltpu.make_async_copy(wk_ref.at[:, pl.ds(at, 128)], wk, sems.at[3]),
        pltpu.make_async_copy(wv_ref.at[:, pl.ds(at, 128)], wv, sems.at[4]),
    ]
    for copy in copies:
        copy.start()
    rows = wk.shape[0]
    slots = ids_ref.shape[1]
    prod[...] = jnp.zeros(prod.shape, F32)
    sub, lane = iota((8, 128), 0), iota((8, 128), 1)
    mine = jnp.where(lane // 64 == sub % 2, 1.0, 0.0).astype(BF16)
    for copy in copies[2:]:
        copy.wait()
    q = q_scr[pl.ds(2 * chip, 2), :]
    prod[0:rows, :] = wk[...].astype(F32) * jnp.concatenate([q[0:1], q[1:2]], axis=1)
    parts = [lax.dot_general(mine, part.astype(BF16), NT, preferred_element_type=F32) for part in split3(prod[...])]
    fold = parts[0] + parts[1] + parts[2]
    top, mid, low = split3(fold)
    part = jnp.where(sub < 2, top, jnp.where(sub < 4, mid, jnp.where(sub < 6, low, 0.0)))
    both = jnp.concatenate([wv[...].astype(F32), part], axis=0).astype(BF16)
    each = stage.shape[0]
    for d in range(each):
        stage[d] = both
    sends = [
        pltpu.make_async_copy(stage, w_ref.at[pl.ds(each * i, each)], sems.at[5 + i])
        for i in range(w_ref.shape[0] // each)
    ]
    for send in sends:
        send.start()

    for copy in copies[:2]:
        copy.wait()
    own = iota((8, slots), 0) == iota((8, slots), 1)
    meta = jnp.sum(jnp.where(own, ids[...].astype(F32), 0.0), axis=1, keepdims=True)
    meta = jnp.broadcast_to(meta, (8, 128))
    n = 4 * slots
    for half in range(2):
        chunk[32 * half + n : 32 * half + 32, :] = meta
    for s in range(slots):
        x = pix[0, s].astype(F32)
        for half in range(2):
            chunk[32 * half + 4 * s : 32 * half + 4 * s + 4, :] = x[:, 128 * half : 128 * half + 128]
    send_ref[...] = chunk[...].astype(BF16)
    for send in sends:
        send.wait()


def table_kernel(pw_ref, ve_ref, gain_ref, bias_ref, rows_ref, gram_ref, ac):
    n_pw, width = pw_ref.shape
    n_ve = ve_ref.shape[0]
    total = rows_ref.shape[0]
    at = n_pw + 4
    gain = gain_ref[...]

    def centered(x):
        return x - jnp.mean(x, axis=-1, keepdims=True)

    pw = centered(pw_ref[...].astype(F32))
    tiles = width // 128
    for i in range(tiles):
        ac[i, 0:n_pw, :] = pw[:, 128 * i : 128 * i + 128]
    ve = centered(ve_ref[...].astype(F32))
    pw = jnp.concatenate([pw * gain, jnp.zeros((at - n_pw, width), F32)], axis=0)
    rows_ref[0:at, :] = pw.astype(BF16)
    rest = jnp.zeros((total - at - n_ve - 1, width), F32)
    rows_ref[at:, :] = jnp.concatenate([ve * gain, bias_ref[...], rest], axis=0).astype(BF16)

    sums = [jnp.zeros((n_ve, 128), F32) for _ in PAIRS]
    for i in range(tiles):
        planes = [ac[i, pl.ds(k, n_ve, stride=4), :] for k in range(4)] + [ve[:, 128 * i : 128 * i + 128]]
        sums = [total + planes[k] * planes[l] for total, (k, l) in zip(sums, PAIRS, strict=True)]
    lane = iota((n_ve, 128), 1)
    gram = jnp.zeros((n_ve, 128), F32)
    for i, (k, l) in enumerate(PAIRS):
        g = jnp.sum(sums[i], axis=-1, keepdims=True) * ((1.0 if k == l else 2.0) / width)
        gram = jnp.where(lane == i, g, gram)
    top, mid, low = split3(gram)
    gram = top + pltpu.roll(mid, 16, 1) + pltpu.roll(low, 32, 1)
    gram_ref[...] = jnp.zeros(gram_ref.shape, BF16)
    gram_ref[0:n_ve, :] = gram.astype(BF16)


def slots_kernel(count_ref, got_ref, gram_ref, out_ref):
    n_chip = got_ref.shape[0]
    slots = 12 * n_chip
    x = got_ref[...].reshape(2 * n_chip, 2, 32, 128)
    x = jnp.concatenate([x[:, i].reshape(64 * n_chip, 128) for i in range(2)], axis=1)
    n = iota((slots, x.shape[0]), 0)
    group = (n * 43) >> 8
    within = n - group * 6
    col = iota(n.shape, 1) - group * 32
    hits = [col == within * 4 + k for k in range(4)] + [col == 24 + within]
    moved = jnp.dot(picked(hits), x, preferred_element_type=F32)
    c = [moved[k * slots : (k + 1) * slots] for k in range(4)]
    meta = moved[4 * slots :, :128]
    ids = meta[:, 0:1].astype(jnp.int32)
    n_ve = gram_ref.shape[0]
    gram = jnp.dot(picked([iota((slots, n_ve), 1) == ids]), gram_ref[...], preferred_element_type=F32)
    gram = gram + pltpu.roll(gram, 112, 1) + pltpu.roll(gram, 96, 1)

    def g(k, l):
        i = PAIRS.index((k, l))
        return gram[:, i : i + 1]

    spread = g(4, 4)
    for k in range(4):
        inner = g(k, 4)
        for l in range(k, 4):
            inner = inner + g(k, l) * c[l]
        spread = spread + c[k] * inner
    r = lax.rsqrt(jnp.maximum(spread, 0.0) + 1e-05)
    top = r.astype(BF16)
    planes = [plane.astype(BF16) for plane in c] + [top, (r - top.astype(F32)).astype(BF16)]
    at = 0
    for plane in planes:
        for half in range(2):
            out_ref[at : at + slots, :] = plane[:, 128 * half : 128 * half + 128]
            at += slots
    meta = jnp.where(iota(meta.shape, 1) == 1, count_ref[0].astype(F32), meta)
    out_ref[at : at + slots, :] = meta.astype(BF16)
    at += slots
    out_ref[at:, :] = jnp.zeros((out_ref.shape[0] - at, 128), BF16)


def attend_kernel(rows_ref, weights_ref, planes_ref, out_ref, wide, w_scr):
    half = lax.axis_index("core")
    n_dp = weights_ref.shape[1]
    rows = weights_ref.shape[2] - 8
    per = 128 // rows
    for d in range(n_dp):
        wide[d * rows : (d + 1) * rows, 0:128] = weights_ref[0, d, 0:rows, :]
    for i in range(n_dp // per):
        tile = jnp.zeros((8, 128), F32)
        for p in range(per):
            piece = weights_ref[0, i * per + p, rows : rows + 8, :].astype(F32)
            tile = tile + (pltpu.roll(piece, rows * p, 1) if p else piece)
        tile = jnp.concatenate([tile, jnp.zeros((120, 128), F32)], axis=0)
        wide[128 * i : 128 * i + 128, 128:256] = tile.T.astype(BF16)
    w = wide[...]
    t = jnp.dot(rows_ref[...], w, preferred_element_type=F32)
    values, keys = t[:, :128], t[:, 128:]
    top, mid, low = split3(keys)
    parts = top + pltpu.roll(mid, 8, 1) + pltpu.roll(low, 16, 1)
    table = jnp.concatenate([values, parts], axis=1).astype(BF16)

    slots = w_scr.shape[0] // 5
    entries = rows_ref.shape[0]
    at = entries - 96

    def plane(i):
        return jnp.concatenate(
            [planes_ref[1, (2 * i + h) * slots : (2 * i + h + 1) * slots, :].astype(F32) for h in range(2)], axis=1
        )

    meta = planes_ref[1, 12 * slots : 13 * slots, :].astype(F32)
    ids = meta[:, 0:1].astype(jnp.int32)
    col = iota((slots, entries), 1)
    found = jnp.dot(
        picked([col == 4 * ids + k for k in range(4)] + [col == at + ids]), table, preferred_element_type=F32
    )
    lane = iota((1, 128), 1)
    key_lanes = jnp.where(lane % 2 == half, 0.125, 0.0)
    value_lanes = jnp.where(lane // 64 == half, 1.0, 0.0)
    v = (found[:, :128] * value_lanes).astype(BF16)
    keyed = jnp.sum(found[:, 128:] * key_lanes, axis=1, keepdims=True)
    key_bias = jnp.sum(keys[at + 91 : at + 92] * key_lanes, axis=1, keepdims=True)
    value_bias = values[at + 91 : at + 92] * value_lanes

    c = [plane(k) for k in range(4)]
    r = plane(4) + plane(5)
    dots = keyed[4 * slots :]
    for k in range(4):
        dots = dots + c[k] * keyed[k * slots : (k + 1) * slots]
    scores = r * dots + key_bias
    scores = jnp.where(iota(scores.shape, 0) < meta[:, 1:2].astype(jnp.int32), scores, -1e30)
    peak = jnp.max(scores, axis=0, keepdims=True)
    expo = jnp.exp(scores - peak)
    share = expo * (1.0 / jnp.sum(expo, axis=0, keepdims=True)) * r
    for k in range(4):
        w_scr[k * slots : (k + 1) * slots, :] = (share * c[k]).astype(BF16)
    w_scr[4 * slots :, :] = share.astype(BF16)
    mixed = lax.dot_general(v, w_scr[...], TN, preferred_element_type=F32).T
    mixed = mixed + value_bias
    turned = pltpu.roll(mixed, 64, 1)
    first = jnp.where(half == 0, mixed, turned).reshape(-1, 2, 8, 128)
    second = jnp.where(half == 0, turned, mixed).reshape(-1, 2, 8, 128)
    left = iota((first.shape[0], 8, 128), 2) < 64
    out_ref[...] = jnp.where(left, first[:, 0], second[:, 1]).astype(BF16)


def project_out_kernel(m_ref, wo_ref, out_ref):
    left = iota((8, 128), 1) < 64
    parts = []
    for i in range(m_ref.shape[0] // 2):
        a, b = m_ref[2 * i].astype(F32), m_ref[2 * i + 1].astype(F32)
        first = jnp.where(left, a, pltpu.roll(b, 64, 1))
        second = jnp.where(left, pltpu.roll(a, 64, 1), b)
        parts.append(jnp.concatenate([first, second], axis=0))
    mixed = jnp.concatenate(parts, axis=1).astype(BF16)
    out_ref[...] = jnp.dot(mixed, wo_ref[...], preferred_element_type=F32).astype(BF16)


def cost(flops, moved):
    return pl.CostEstimate(flops=flops, transcendentals=0, bytes_accessed=moved)


def on_device(
    pixels,
    var_ids,
    counts,
    patch_weight,
    var_embed,
    norm_gain,
    norm_bias,
    key_weight,
    value_weight,
    query,
    out_weight,
):
    slots, pp, patches = pixels.shape[1:]
    n_var, width = var_embed.shape
    n_dp = lax.axis_size(DP)
    n_chip, n_core = lax.axis_size("y"), lax.axis_size("core")
    n_sv = n_chip * n_core
    all_slots = slots * n_sv
    entries = 464
    rows = key_weight.shape[0] + 8
    smem, vmem = whole(pltpu.SMEM), whole()

    packed_w, packed_x = pl.pallas_call(
        pack_kernel,
        out_shape=(jax.ShapeDtypeStruct((n_dp, rows, 128), BF16), pltpu.VMEM((64, 128), BF16)),
        in_specs=[whole(pltpu.HBM)] * 5,
        out_specs=(whole(pltpu.HBM), vmem),
        scratch_shapes=[
            pltpu.VMEM((rows - 8, 128), BF16),
            pltpu.VMEM((rows - 8, 128), BF16),
            pltpu.VMEM(query.shape, F32),
            pltpu.VMEM(pixels.shape, BF16),
            pltpu.VMEM(var_ids.shape, jnp.int32),
            pltpu.VMEM((128, 128), F32),
            pltpu.VMEM((64, 128), F32),
            pltpu.VMEM((n_dp // 4, rows, 128), BF16),
            pltpu.SemaphoreType.DMA((9,)),
        ],
        name="pack",
    )(var_ids, key_weight, value_weight, query, pixels)
    of_chip = lax.all_gather(packed_x, "core")

    def tables(patch_weight, var_embed, norm_gain, norm_bias):
        return pl.pallas_call(
            table_kernel,
            out_shape=(
                jax.ShapeDtypeStruct((entries, width), BF16),
                jax.ShapeDtypeStruct((96, 128), BF16),
            ),
            in_specs=[vmem] * 4,
            out_specs=(vmem,) * 2,
            scratch_shapes=[pltpu.VMEM((width // 128, n_var * pp + 4, 128), F32)],
            cost_estimate=cost(20 * entries * width, 8 * entries * width),
            compiler_params=pltpu.CompilerParams(vmem_limit_bytes=24 << 20),
            name="tables",
        )(
            patch_weight.reshape(n_var * pp, width),
            var_embed,
            norm_gain.reshape(1, width),
            norm_bias.reshape(1, width),
        )

    def weights_of_all(packed_w, of_chip, counts, *params):
        table, _ = tables(*params)
        return lax.all_to_all(packed_w, DP, 0, 0, tiled=True), table

    def slots_of_all(packed_w, of_chip, counts, *params):
        table, gram = tables(*params)
        send = jnp.broadcast_to(of_chip, (n_chip, *of_chip.shape))
        planes = pl.pallas_call(
            slots_kernel,
            out_shape=jax.ShapeDtypeStruct((n_dp * rows, 128), BF16),
            in_specs=[smem, vmem, vmem],
            out_specs=vmem,
            compiler_params=pltpu.CompilerParams(vmem_limit_bytes=24 << 20),
            name="slots",
        )(counts, lax.all_to_all(send, "y", 0, 0, tiled=True), gram)
        return planes.reshape(n_dp, rows, 128), table

    params = (counts, patch_weight, var_embed, norm_gain, norm_bias)
    mine, table = lax.cond(lax.axis_index("core") == 0, weights_of_all, slots_of_all, packed_w, of_chip, *params)
    both = lax.all_gather(mine, "core")

    mixed = pl.pallas_call(
        attend_kernel,
        out_shape=jax.ShapeDtypeStruct((n_sv, 8, 128), BF16),
        in_specs=[vmem] * 3,
        out_specs=vmem,
        scratch_shapes=[pltpu.VMEM((width, 256), BF16), pltpu.VMEM((5 * all_slots, patches), BF16)],
        compiler_params=pltpu.CompilerParams(vmem_limit_bytes=24 << 20),
        name="attend",
    )(table, both, both.reshape(n_core, n_dp * rows, 128))
    owned = lax.all_to_all(mixed, VAR, 0, 0, tiled=True)

    out = pl.pallas_call(
        project_out_kernel,
        out_shape=jax.ShapeDtypeStruct((patches // n_sv, width), BF16),
        in_specs=[vmem, vmem],
        out_specs=vmem,
        compiler_params=pltpu.CompilerParams(vmem_limit_bytes=16 << 20),
        name="project_out",
    )(owned, out_weight)
    return out[None]


def solution(mesh):
    torus = Mesh(mesh.devices.reshape(4, 8, 8, 2), (*DP, *VAR))
    return jax.shard_map(
        on_device,
        mesh=torus,
        in_specs=(
            P(DP, VAR, None, None),
            P(DP, VAR),
            P(DP),
            P(),
            P(),
            P(),
            P(),
            P(DP, None),
            P(DP, None),
            P(),
            P(),
        ),
        out_specs=P(DP, VAR, None),
        check_vma=False,
    )
```
